32 devices in a mesh: mom: 8 (over z, core), bond: 4 (over y, x).
Axes of the slice: x: 2, y: 2, z: 4, core: 2. Of those that a mesh axis runs over, the one named last changes fastest.
Arguments:
- vertex: bfloat16 [3, 256, 512, 512], P(None, ('mom', 'bond')), may hold values from -6 to 6
- loop_matrix: bfloat16 [3, 256, 512, 512], P(None, ('mom', 'bond')), may hold values from -0.01171875 to 0.01171875
- own_mix: float32 [3, 3], replicated, may hold values from -4 to 4
- cross_mix: float32 [3, 3], replicated, may hold values from -4 to 4
- shells: int32 [512], replicated, may hold values from 0 to 4
- partner: int32 [512], replicated, may hold values from 0 to 511, as said below
- grid_index: int32 [256], replicated, may hold values from 0 to 255, each once
Outputs:
- flowed: bfloat16 [3, 256, 512, 512], P(None, ('mom', 'bond'))
The draws below stay inside these ranges and needn't reach their ends.
Inputs may be any that keep to these rules, and one draw needn't show every extreme that they name: partner[partner[a]] = a and partner[a] != a for every bond a; partner[a] // 64 = (a // 64 + 512 // 128) % 8. `grid_index`: each grid point appears once; point k has coordinates (k // 16, k % 16).
All inputs are finite; a program needn't handle non-finite values.
Results may differ from the reference program's by a relative error of at most 0.007.
Values may be sent and summed in bfloat16 or wider, within the bound.
A program may use at most 256 MiB of HBM per device.

```python
import math
import jax
import jax.numpy as jnp
from jax import lax

G = 16
NB = 512
NCH = 3
SHELLS = 5
Q = 256
PB = 64


def draw_partner(key, part):
    half_blocks = NB // PB // 2
    scores = jax.random.randint(key, (half_blocks, PB), 0, 1 << 20) * PB + jnp.arange(PB, dtype=jnp.int32)[None, :]
    sigma_order = jnp.argsort(scores, axis=1).astype(jnp.int32)
    inverse = jnp.argsort(sigma_order, axis=1).astype(jnp.int32)
    block_ids = jnp.arange(half_blocks, dtype=jnp.int32)[:, None]
    lower_half = (block_ids + half_blocks) * PB + sigma_order
    upper_half = block_ids * PB + inverse
    return jnp.concatenate([lower_half.reshape(-1), upper_half.reshape(-1)]).astype(jnp.int32)


def place_ends(values, key, smallest, top_value):
    extent = values.shape
    index_at = [jax.random.randint(jax.random.fold_in(key, axis), (), 0, extent[axis]) for axis in range(len(extent))]
    values = values.at[tuple(index_at)].set(smallest)
    longest = extent.index(max(extent))
    index_at[longest] = (index_at[longest] + 1) % extent[longest]
    return values.at[tuple(index_at)].set(top_value)


def block_scale(key, extent, cuts, least, top_value):
    gain, own = 1.0, jax.random.fold_in(key, 6)
    for dim, blocks in cuts:
        draws = jnp.exp(jax.random.uniform(jax.random.fold_in(own, dim), (blocks,), jnp.float32, least / len(cuts), top_value / len(cuts)))
        gain = gain * jnp.repeat(draws, extent[dim] // blocks).reshape([-1 if axis == dim else 1 for axis in range(len(extent))])
    return gain


def noise(stream_key, dims, width, limit, cuts=(), held_as=jnp.bfloat16):
    loudness = block_scale(stream_key, dims, cuts, -0.22, 0.18) if cuts else 1.0
    result = jax.random.normal(stream_key, dims, jnp.float32) * width * loudness
    return jnp.minimum(jnp.maximum(result, -limit), limit).astype(held_as)


def setup_inputs(seed: int = 0) -> dict:
    key_list = jax.random.split(jax.random.key(seed), 8)
    vertex = noise(key_list[0], (NCH, Q, NB, NB), 1.0, 6.0, ((1, 32),))
    loop_matrix = noise(key_list[1], (NCH, Q, NB, NB), (NB * NB) ** -0.5, 0.01171875, ((1, 32),))
    own_mix = noise(key_list[2], (NCH, NCH), 1.0, 4.0, (), jnp.float32)
    cross_mix = noise(key_list[3], (NCH, NCH), 1.0, 4.0, (), jnp.float32)
    shells = place_ends(jax.random.randint(key_list[4], (NB,), 0, SHELLS), jax.random.fold_in(key_list[4], 1), 0, SHELLS - 1).astype(jnp.int32)
    partner = draw_partner(jax.random.fold_in(key_list[7], 71), 0)
    grid_index = jax.random.permutation(key_list[6], Q).astype(jnp.int32)
    return {"vertex": vertex, "loop_matrix": loop_matrix, "own_mix": own_mix, "cross_mix": cross_mix, "shells": shells, "partner": partner, "grid_index": grid_index}


def cas_table(grid_index, negate):
    points = jnp.arange(Q, dtype=jnp.int32)
    disp_x = points // G
    disp_y = points % G
    wave_x = grid_index // G
    wave_y = grid_index % G
    phases = (disp_x[:, None] * wave_x[None, :] + disp_y[:, None] * wave_y[None, :]) % G
    if negate:
        phases = (G - phases) % G
    angles = phases.astype(jnp.float32) * (2.0 * math.pi / G)
    return (jnp.cos(angles) + jnp.sin(angles)).astype(jnp.bfloat16)


def cycle_index():
    points = jnp.arange(Q, dtype=jnp.int32)
    centre_x = (points // G + G // 2) % G - G // 2
    centre_y = (points % G + G // 2) % G - G // 2
    return jnp.maximum(jnp.abs(centre_x), jnp.abs(centre_y))


def reference(vertex, loop_matrix, own_mix, cross_mix, shells, partner, grid_index):
    def flow_step(operands):
        vertex_one, loop_one = operands
        vertex_wide = vertex_one.astype(jnp.float32)
        half_product = jnp.einsum("qab,qbd->qad", vertex_wide, loop_one.astype(jnp.float32)).astype(jnp.bfloat16)
        return jnp.einsum("qab,qbd->qad", half_product.astype(jnp.float32), vertex_wide)

    product = lax.map(flow_step, (vertex, loop_matrix))
    rounded = product.astype(jnp.bfloat16)
    crossed = jnp.take(jnp.take(rounded, partner, axis=2), partner, axis=3)
    plus_table = cas_table(grid_index, False).astype(jnp.float32)
    minus_table = cas_table(grid_index, True).astype(jnp.float32)
    cycle_values = cycle_index()
    height = math.gcd(NB, 64)
    block_count = NB // height
    row_width = height * NB

    def by_rows(field_data):
        return jnp.moveaxis(field_data.reshape(NCH, Q, block_count, height, NB), 2, 0)

    def lattice_step(operands):
        own_rows, cross_rows, shell_rows = operands
        own_lattice = jnp.einsum("rq,cqe->cre", plus_table, own_rows.reshape(NCH, Q, row_width).astype(jnp.float32), precision=lax.Precision.HIGHEST)
        cross_lattice = jnp.einsum("rq,cqe->cre", minus_table, cross_rows.reshape(NCH, Q, row_width).astype(jnp.float32), precision=lax.Precision.HIGHEST)
        mixed_terms = jnp.einsum("dc,cre->dre", own_mix, own_lattice, precision=lax.Precision.HIGHEST) + jnp.einsum("dc,cre->dre", cross_mix, cross_lattice, precision=lax.Precision.HIGHEST)
        reach_sum = (shell_rows[:, None] + shells[None, :]).reshape(row_width)
        kept_mask = cycle_values[:, None] <= reach_sum[None, :]
        projected = jnp.where(kept_mask[None], mixed_terms * (1.0 / Q), 0.0).astype(jnp.bfloat16)
        returned = jnp.einsum("rq,dre->dqe", plus_table, projected.astype(jnp.float32), precision=lax.Precision.HIGHEST)
        return returned.astype(jnp.bfloat16)

    pieces = lax.map(lattice_step, (by_rows(rounded), by_rows(crossed), shells.reshape(block_count, height)))
    returned = jnp.moveaxis(pieces.reshape(block_count, NCH, Q, height, NB), 0, 2).reshape(NCH, Q, NB, NB)
    flowed = vertex.astype(jnp.float32) + product + returned.astype(jnp.float32)
    return flowed.astype(jnp.bfloat16)
```

```python
import functools
import math

import jax
import jax.numpy as jnp
import numpy as np
from jax import lax
from jax.experimental import pallas as pl
from jax.experimental.layout import Layout, with_layout_constraint
from jax.experimental.pallas import tpu as pltpu
from jax.sharding import PartitionSpec as P

LANES = 128
PAIR = 2
ROWS = 2
VMEM_LIMIT = 58 * 1024 * 1024
AXES = ("mom", "bond")


def cas_table(grid_index, negate):
    count = grid_index.shape[0]
    side = math.isqrt(count)
    points = jnp.arange(count, dtype=jnp.int32)
    disp_x = points // side
    disp_y = points % side
    wave_x = grid_index // side
    wave_y = grid_index % side
    phases = (disp_x[:, None] * wave_x[None, :] + disp_y[:, None] * wave_y[None, :]) % side
    if negate:
        phases = (side - phases) % side
    angles = phases.astype(jnp.float32) * (2.0 * math.pi / side)
    return (jnp.cos(angles) + jnp.sin(angles)).astype(jnp.bfloat16)


def cycle_index(count):
    side = math.isqrt(count)
    points = jnp.arange(count, dtype=jnp.int32)
    centre_x = (points // side + side // 2) % side - side // 2
    centre_y = (points % side + side // 2) % side - side // 2
    return jnp.maximum(jnp.abs(centre_x), jnp.abs(centre_y))


def dot(a, b):
    return jnp.dot(a, b, preferred_element_type=jnp.float32)


def product_kernel(mom_local, places, vertex_ref, loop_ref, pick_ref, spread_ref, *refs):
    base_ref, send_ref, token_ref, wide_ref = refs[-4:]
    step = pl.program_id(1)
    token_ref[...] = jnp.zeros_like(token_ref)
    vertex = vertex_ref[0, 0]
    bonds = vertex.shape[0]
    half = bonds // 2
    group = half // places
    half_product = dot(vertex, loop_ref[0, 0]).astype(jnp.bfloat16)
    product = dot(half_product, vertex)
    base_ref[0, 0] = (product + vertex.astype(jnp.float32)).astype(jnp.bfloat16)
    rounded = product.astype(jnp.bfloat16)
    left = rounded[:, :half]
    right = dot(rounded[:, half:], spread_ref[...]).astype(jnp.bfloat16)
    for side, part in enumerate((left, right)):
        upper = dot(pick_ref[...], part[half:])
        lower = part[:half].astype(jnp.float32)
        for lane in range(half // LANES):
            at = side * (half // LANES) + lane
            cols = slice(lane * LANES, (lane + 1) * LANES)
            if mom_local == 1:
                wide_ref[at, :half] = lower[:, cols]
                wide_ref[at, half:] = upper[:, cols]
            else:
                wide_ref[at, pl.ds(step, half, stride=mom_local), :] = lower[:, cols]
                wide_ref[at, pl.ds(half * mom_local + step, half, stride=mom_local), :] = upper[:, cols]

    @pl.when(step == mom_local - 1)
    def _():
        for at in range(bonds // LANES):
            cols = slice(at * LANES, (at + 1) * LANES)
            for side in range(2):
                piece = wide_ref[at, side * half * mom_local : (side + 1) * half * mom_local]
                send_ref[:, 0, side, :, :, cols] = piece.reshape(places, group, mom_local, LANES).astype(jnp.bfloat16)


def first_product_kernel(places, vertex_ref, loop_ref, pick_ref, spread_ref, base_ref, send_ref, token_ref):
    token_ref[...] = jnp.zeros_like(token_ref)
    bonds = vertex_ref.shape[-1]
    half = bonds // 2
    group = half // places
    for n in range(vertex_ref.shape[1]):
        vertex = vertex_ref[0, n]
        half_product = dot(vertex, loop_ref[0, n]).astype(jnp.bfloat16)
        product = dot(half_product, vertex)
        base_ref[0, n] = (product + vertex.astype(jnp.float32)).astype(jnp.bfloat16)
        rounded = product.astype(jnp.bfloat16)
        left = rounded[:, :half]
        right = dot(rounded[:, half:], spread_ref[...]).astype(jnp.bfloat16)
        for side, part in enumerate((left, right)):
            cols = slice(side * half, (side + 1) * half)
            lower = part[:half].astype(jnp.float32)
            upper = dot(pick_ref[...], part[half:])
            send_ref[:, 0, n, 0, :, cols] = lower.reshape(places, group, half).astype(jnp.bfloat16)
            send_ref[:, 0, n, 1, :, cols] = upper.reshape(places, group, half).astype(jnp.bfloat16)


def lattice_kernel(sizes, targets, own_ref, cross_ref, plus_ref, minus_ref, back_ref, cycle_ref, reach_ref, *refs):
    received = [(refs[k], n) for k, size in enumerate(sizes) for n in range(size)]
    send_ref = refs[-1]
    places, _, _, _, mom_local, bonds = send_ref.shape
    count = places * mom_local
    half = bonds // 2
    for row in range(send_ref.shape[3]):
        blocks = [
            [
                ref[:, n, side, row].astype(jnp.float32).reshape(count, bonds).astype(jnp.bfloat16)
                for side in range(2)
            ]
            for ref, n in received
        ]
        for side in range(2):
            mixed = [None] * len(targets)
            for c in range(len(received)):
                own = dot(plus_ref[...], blocks[c][side])
                crossed = dot(minus_ref[...], blocks[c][1 - side])
                crossed = jnp.concatenate([crossed[:, half:], crossed[:, :half]], axis=1)
                for k, d in enumerate(targets):
                    term = own_ref[d, c] * own + cross_ref[d, c] * crossed
                    mixed[k] = term if c == 0 else mixed[k] + term
            kept = cycle_ref[...] <= reach_ref[side, row]
            for k in range(len(targets)):
                projected = jnp.where(kept, mixed[k], 0.0).astype(jnp.bfloat16)
                returned = dot(back_ref[...], projected)
                send_ref[:, k, side, row] = returned.reshape(places, mom_local, bonds).astype(jnp.bfloat16)


def finish_kernel(mom_local, base_ref, received_ref, pick_ref, spread_ref, out_ref, wide_ref):
    step = pl.program_id(1)
    places, _, _, group, _, bonds = received_ref.shape
    half = bonds // 2

    @pl.when(step == 0)
    def _():
        for at in range(bonds // LANES):
            cols = slice(at * LANES, (at + 1) * LANES)
            for side in range(2):
                piece = received_ref[:, 0, side, :, :, cols].astype(jnp.float32)
                wide_ref[at, side * half * mom_local : (side + 1) * half * mom_local] = piece.reshape(
                    half * mom_local, LANES
                )

    def rows_of(at):
        if mom_local == 1:
            return wide_ref[at]
        return wide_ref[at, pl.ds(step, bonds, stride=mom_local), :]

    tiles = half // LANES
    left = jnp.concatenate([rows_of(at) for at in range(tiles)], axis=1)
    right = jnp.concatenate([rows_of(at) for at in range(tiles, 2 * tiles)], axis=1)
    right = dot(right.astype(jnp.bfloat16), pick_ref[...])
    for side, part in enumerate((left, right)):
        cols = slice(side * half, (side + 1) * half)
        lower = part[:half]
        upper = dot(spread_ref[...], part[half:].astype(jnp.bfloat16))
        out_ref[0, 0, :half, cols] = (base_ref[0, 0, :half, cols].astype(jnp.float32) + lower).astype(jnp.bfloat16)
        out_ref[0, 0, half:, cols] = (base_ref[0, 0, half:, cols].astype(jnp.float32) + upper).astype(jnp.bfloat16)


def last_finish_kernel(base_ref, received_ref, pick_ref, spread_ref, out_ref):
    bonds = base_ref.shape[-1]
    half = bonds // 2
    for n in range(base_ref.shape[1]):
        for side in range(2):
            cols = slice(side * half, (side + 1) * half)
            lower = received_ref[:, 0, n, 0, :, cols].astype(jnp.float32).reshape(half, half)
            upper = received_ref[:, 0, n, 1, :, cols].astype(jnp.float32).reshape(half, half).astype(jnp.bfloat16)
            if side:
                lower = dot(lower.astype(jnp.bfloat16), pick_ref[...])
                upper = dot(upper, pick_ref[...]).astype(jnp.bfloat16)
            upper = dot(spread_ref[...], upper)
            out_ref[0, n, :half, cols] = (base_ref[0, n, :half, cols].astype(jnp.float32) + lower).astype(jnp.bfloat16)
            out_ref[0, n, half:, cols] = (base_ref[0, n, half:, cols].astype(jnp.float32) + upper).astype(jnp.bfloat16)


def whole(shape):
    return pl.BlockSpec(shape, lambda *steps: (0,) * len(shape))


def params(axes):
    return pltpu.CompilerParams(dimension_semantics=("arbitrary",) * axes, vmem_limit_bytes=VMEM_LIMIT)


def general_flow(vertex, loop_matrix, own_mix, cross_mix, shells, partner, grid_index):
    places = lax.axis_size("mom") * lax.axis_size("bond")
    place = lax.axis_index("mom") * lax.axis_size("bond") + lax.axis_index("bond")
    channels, mom_local, bonds, _ = vertex.shape
    count = grid_index.shape[0]
    half = bonds // 2
    group = half // places
    tiles = bonds // LANES
    bf16 = jnp.bfloat16
    first = list(range(channels))
    send_groups = [first[:1], first[1:]]
    back_groups = [first[:-1], first[-1:]]

    lower_partner = partner[:half] - half
    uppers = jnp.arange(half, dtype=jnp.int32)
    pick = (lower_partner[:, None] == uppers[None, :]).astype(bf16)
    spread = pick.T

    wide = pltpu.VMEM((tiles, bonds * mom_local, LANES), jnp.float32)
    square = (half, half)
    matmul = 2 * mom_local * bonds**3
    field_bytes = 2 * mom_local * bonds * bonds
    field = jax.ShapeDtypeStruct(vertex.shape, bf16)
    token_shape = jax.ShapeDtypeStruct((8, LANES), jnp.float32)

    def flow(members):
        return jax.ShapeDtypeStruct((places, members, 2, group, mom_local, bonds), bf16)

    def one_flow():
        return pl.BlockSpec((places, 1, 2, group, mom_local, bonds), lambda c, i: (0, c, 0, 0, 0, 0))

    def matrix_at(start):
        return pl.BlockSpec((1, 1, bonds, bonds), lambda c, i: (c + start, i, 0, 0))

    def exchange(outgoing):
        return lax.all_to_all(outgoing, AXES, split_axis=0, concat_axis=0, tiled=True)

    pair = PAIR if mom_local % PAIR == 0 else 1
    plain = jax.ShapeDtypeStruct((places, 1, mom_local, 2, group, bonds), bf16)
    plain_block = pl.BlockSpec((places, 1, pair, 2, group, bonds), lambda i: (0, 0, i, 0, 0, 0))

    def pair_at(start):
        return pl.BlockSpec((1, pair, bonds, bonds), lambda i: (start, i, 0, 0))

    base, outgoing, token = pl.pallas_call(
        functools.partial(first_product_kernel, places),
        grid=(mom_local // pair,),
        in_specs=[pair_at(0), pair_at(0), whole(square), whole(square)],
        out_specs=[pair_at(0), plain_block, whole(token_shape.shape)],
        out_shape=[field, plain, token_shape],
        compiler_params=params(1),
        cost_estimate=pl.CostEstimate(flops=5 * matmul // 2, bytes_accessed=4 * field_bytes, transcendentals=0),
        name="product_first",
    )(vertex, loop_matrix, pick, spread)
    whole_rows = with_layout_constraint(exchange(outgoing), Layout(major_to_minor=tuple(range(6))))
    arrived = [whole_rows.transpose(0, 1, 3, 4, 2, 5)]
    for members in send_groups[1:]:
        matrix = matrix_at(members[0])
        size = len(members)
        base, outgoing, _ = pl.pallas_call(
            functools.partial(product_kernel, mom_local, places),
            grid=(size, mom_local),
            in_specs=[matrix, matrix, whole(square), whole(square)]
            + [pl.BlockSpec(memory_space=pl.ANY)],
            out_specs=[matrix, one_flow(), whole(token_shape.shape)],
            out_shape=[field, flow(size), token_shape],
            input_output_aliases={4: 0},
            scratch_shapes=[wide],
            compiler_params=params(2),
            cost_estimate=pl.CostEstimate(
                flops=5 * size * matmul // 2, bytes_accessed=4 * size * field_bytes, transcendentals=0
            ),
            name="product_%d" % members[0],
        )(vertex, loop_matrix, pick, spread, base)
        arrived.append(exchange(outgoing))

    shells, partner, grid_index, own_mix, cross_mix, _ = lax.optimization_barrier(
        (shells, partner, grid_index, own_mix, cross_mix, token)
    )
    plus_table = cas_table(grid_index, False)
    minus_table = cas_table(grid_index, True)
    back_table = plus_table.T
    cycle = cycle_index(count)[:, None]
    shell_order = jnp.concatenate([shells[:half], jnp.take(shells, partner[:half])])
    shell_rows = lax.dynamic_slice_in_dim(shell_order.reshape(2, half), place * group, group, axis=1)
    reach = (shell_rows[:, :, None] + shell_order[None, None, :]).reshape(2, group, 1, bonds)
    own_scaled = own_mix * (1.0 / count)
    cross_scaled = cross_mix * (1.0 / count)

    rows = ROWS if group % ROWS == 0 else 1

    def row_block(members):
        return pl.BlockSpec((places, members, 2, rows, mom_local, bonds), lambda i: (0, 0, 0, i, 0, 0))

    table = whole((count, count))
    scalars = pl.BlockSpec(memory_space=pltpu.SMEM)
    sizes = [len(members) for members in send_groups]
    finished, earlier = [], []
    for members in back_groups:
        size = len(members)
        outgoing = pl.pallas_call(
            functools.partial(lattice_kernel, sizes, members),
            grid=(group // rows,),
            in_specs=[
                scalars,
                scalars,
                table,
                table,
                table,
                whole((count, 1)),
                pl.BlockSpec((2, rows, 1, bonds), lambda i: (0, i, 0, 0)),
            ]
            + [row_block(n) for n in sizes]
            + [pl.BlockSpec(memory_space=pl.ANY)] * len(earlier),
            out_specs=row_block(size),
            out_shape=flow(size),
            compiler_params=params(1),
            cost_estimate=pl.CostEstimate(
                flops=(2 * channels + size) * 2 * count * count * 2 * group * bonds,
                bytes_accessed=(channels + size) * field_bytes,
                transcendentals=0,
            ),
            name="lattice_%d" % members[0],
        )(own_scaled, cross_scaled, plus_table, minus_table, back_table, cycle, reach, *arrived, *earlier)
        earlier = [outgoing]
        if members is back_groups[-1]:
            outgoing = outgoing.transpose(0, 1, 4, 2, 3, 5)
        finished.append(exchange(outgoing))

    for members, received in zip(back_groups[:-1], finished[:-1]):
        matrix = matrix_at(members[0])
        size = len(members)
        base = pl.pallas_call(
            functools.partial(finish_kernel, mom_local),
            grid=(size, mom_local),
            in_specs=[matrix, one_flow(), whole(square), whole(square)],
            out_specs=matrix,
            out_shape=field,
            input_output_aliases={0: 0},
            scratch_shapes=[wide],
            compiler_params=params(2),
            cost_estimate=pl.CostEstimate(
                flops=size * matmul // 2, bytes_accessed=3 * size * field_bytes, transcendentals=0
            ),
            name="finish_%d" % members[0],
        )(base, received, pick, spread)
    last = back_groups[-1][0]
    return pl.pallas_call(
        last_finish_kernel,
        grid=(mom_local // pair,),
        in_specs=[pair_at(last), plain_block, whole(square), whole(square)],
        out_specs=pair_at(last),
        out_shape=field,
        input_output_aliases={0: 0},
        compiler_params=params(1),
        cost_estimate=pl.CostEstimate(flops=matmul // 2, bytes_accessed=3 * field_bytes, transcendentals=0),
        name="finish_last",
    )(base, finished[-1], pick, spread)


MESH = pl.DeviceIdType.MESH


def flow_kernel(
    parts,
    vertex_ref,
    loop_ref,
    own_ref,
    cross_ref,
    partner_ref,
    shells_ref,
    grid_ref,
    base_ref,
    back_ref,
    send_ref,
    recv_ref,
    wide_ref,
    vertex_buf,
    loop_buf,
    base_buf,
    tile_buf,
    pick_ref,
    spread_ref,
    block_ref,
    plus_ref,
    minus_ref,
    turn_ref,
    cycle_ref,
    row_ref,
    col_ref,
    load_sem,
    store_sem,
    self_sem,
    out_sem,
    in_sem,
    home_sem,
    finish_sem,
):
    bf16, f32 = jnp.bfloat16, jnp.float32
    chunks, channels, places, depth, width = send_ref.shape
    mom_local, bonds = vertex_ref.shape[1], vertex_ref.shape[-1]
    half, count = bonds // 2, places * mom_local
    group = half // places
    pair = 2 * group
    side = math.isqrt(count)
    steps = channels * mom_local
    columns = lax.axis_size("bond")
    place = lax.axis_index("mom") * columns + lax.axis_index("bond")

    def device(offset):
        at = lax.rem(place + offset, places)
        return at, (lax.div(at, columns), lax.rem(at, columns))

    barrier = pltpu.get_barrier_semaphore()

    def greet(offset, carry):
        pl.semaphore_signal(barrier, inc=1, device_id=device(offset)[1], device_id_type=MESH)
        return carry

    lax.fori_loop(1, places, greet, 0)

    def loads(step, slot):
        c, n = lax.div(step, mom_local), lax.rem(step, mom_local)
        return [
            pltpu.make_async_copy(source.at[c, n], target.at[slot], load_sem.at[k, slot])
            for k, (source, target) in enumerate(((vertex_ref, vertex_buf), (loop_ref, loop_buf)))
        ]

    def store(step, slot):
        c, n = lax.div(step, mom_local), lax.rem(step, mom_local)
        return pltpu.make_async_copy(base_buf.at[slot], base_ref.at[c, n], store_sem.at[slot])

    for copy in loads(0, 0):
        copy.start()

    down = lax.broadcasted_iota(jnp.int32, (half, half), 0)
    lower_partner = partner_ref[:, :half] - half
    pick_ref[...] = jnp.where(down == partner_ref[:, half:], 1.0, 0.0).astype(bf16)
    spread_ref[...] = jnp.where(down == lower_partner, 1.0, 0.0).astype(bf16)

    def forward(unit_k, unit_c, first, size):
        unit = unit_k * channels + unit_c

        def one(offset, carry):
            at, target = device(offset)
            rows = pl.ds(first, size)
            pltpu.make_async_remote_copy(
                src_ref=send_ref.at[unit_k, unit_c, at, rows],
                dst_ref=recv_ref.at[unit_k, unit_c, place, rows],
                send_sem=out_sem.at[0, unit],
                recv_sem=in_sem.at[0, unit],
                device_id=target,
                device_id_type=MESH,
            ).start()
            return carry

        lax.fori_loop(1, places, one, 0)

    def backward(unit_k, unit_c):
        unit = unit_k * channels + unit_c

        def one(offset, carry):
            at, target = device(offset)
            pltpu.make_async_remote_copy(
                src_ref=send_ref.at[unit_k, unit_c, at],
                dst_ref=back_ref.at[unit_k, unit_c, place],
                send_sem=out_sem.at[1, unit],
                recv_sem=in_sem.at[1, unit],
                device_id=target,
                device_id_type=MESH,
            ).start()
            return carry

        lax.fori_loop(1, places, one, 0)

    def all_of(way, unit_k, unit_c):
        unit = unit_k * channels + unit_c
        landing = back_ref if way else recv_ref
        return pltpu.make_async_remote_copy(
            src_ref=send_ref.at[unit_k, unit_c, pl.ds(0, places - 1)],
            dst_ref=landing.at[unit_k, unit_c, pl.ds(0, places - 1)],
            send_sem=out_sem.at[way, unit],
            recv_sem=in_sem.at[way, unit],
            device_id=device(1)[1],
            device_id_type=MESH,
        )

    def own_block(way, unit_k, unit_c):
        unit = unit_k * channels + unit_c
        landing, sem = (back_ref, home_sem) if way else (recv_ref, self_sem)
        return pltpu.make_async_copy(
            send_ref.at[unit_k, unit_c, place], landing.at[unit_k, unit_c, place], sem.at[unit]
        )

    part = mom_local // parts

    def product_step(step, carry):
        slot = lax.rem(step, 2)
        c, n = lax.div(step, mom_local), lax.rem(step, mom_local)

        @pl.when(step + 1 < steps)
        def _():
            for copy in loads(step + 1, 1 - slot):
                copy.start()

        for copy in loads(step, slot):
            copy.wait()
        vertex = vertex_buf[slot]
        half_product = dot(vertex, loop_buf[slot]).astype(bf16)
        product = dot(half_product, vertex)
        rounded = product.astype(bf16)
        left = rounded[:, :half]
        right = dot(rounded[:, half:], spread_ref[...]).astype(bf16)
        rows = pl.ds(pl.multiple_of(n * pair, pair), pair)
        for at, piece in enumerate((left, right)):
            upper = dot(pick_ref[...], piece[half:])
            lower = piece[:half].astype(f32)
            for k in range(chunks):
                cols = slice(k * LANES, (k + 1) * LANES)
                both = jnp.concatenate(
                    [lower[:, cols].reshape(places, group, LANES), upper[:, cols].reshape(places, group, LANES)], axis=1
                )
                send_ref[k, c, :, rows, at * LANES : (at + 1) * LANES] = both.astype(bf16)

        @pl.when(step >= 2)
        def _():
            store(step - 2, slot).wait()

        base_buf[slot] = (product + vertex.astype(f32)).astype(bf16)
        store(step, slot).start()

        @pl.when(step == part - 1)
        def _():
            pl.semaphore_wait(barrier, places - 1)

        @pl.when((c == 0) & (lax.rem(n, part) == part - 1))
        def _():
            forward(0, 0, pl.multiple_of((n - part + 1) * pair, part * pair), part * pair)

        @pl.when((c > 0) & (n == mom_local - 1))
        def _():
            forward(0, c, 0, depth)

        return carry

    lax.fori_loop(0, steps, product_step, 0)

    def later_chunk(unit, carry):
        forward(lax.div(unit, channels), lax.rem(unit, channels), 0, depth)
        return carry

    lax.fori_loop(channels, chunks * channels, later_chunk, 0)

    def start_own(unit, carry):
        own_block(0, lax.div(unit, channels), lax.rem(unit, channels)).start()
        return carry

    lax.fori_loop(0, chunks * channels, start_own, 0)
    for step in (steps - 2, steps - 1):
        store(step, step % 2).wait()

    def floor_div(value, by):
        return jnp.floor((value + 0.5) * (1.0 / by))

    points = lax.broadcasted_iota(jnp.int32, (count, count), 0).astype(f32)
    disp_x = floor_div(points, side)
    disp_y = points - side * disp_x
    far = []
    for disp in (disp_x, disp_y):
        moved = disp + side // 2
        far.append(jnp.abs(moved - side * floor_div(moved, side) - side // 2))
    cycle_ref[...] = jnp.maximum(far[0], far[1])
    grid = grid_ref[...].astype(f32)
    wave_x = floor_div(grid, side)
    wave_y = grid - side * wave_x
    phases = disp_x * wave_x + disp_y * wave_y
    phases = phases - side * floor_div(phases, side)
    angles = np.arange(side, dtype=np.float32) * np.float32(2.0 * math.pi / side)
    cas = (np.cos(angles) + np.sin(angles)).astype(np.float32)
    plus = jnp.zeros_like(phases)
    minus = jnp.zeros_like(phases)
    for phase in range(side):
        here = phases == float(phase)
        plus = jnp.where(here, float(cas[phase]), plus)
        minus = jnp.where(here, float(cas[(side - phase) % side]), minus)
    plus_ref[...] = plus.astype(bf16)
    minus_ref[...] = minus.astype(bf16)
    turn_ref[...] = plus.T.astype(bf16)

    shells = shells_ref[...].astype(f32)
    low_shells = shells[:, :half]
    up_shells = dot(jnp.broadcast_to(shells[:, half:], (8, half)).astype(bf16), spread_ref[...])[:1]
    lane = lax.broadcasted_iota(jnp.int32, (group, half), 1)
    mine = lane == place * group + lax.broadcasted_iota(jnp.int32, (group, half), 0)
    for s, line in enumerate((low_shells, up_shells)):
        column = jnp.sum(jnp.where(mine, jnp.broadcast_to(line, (group, half)), 0.0), axis=1, keepdims=True)
        row_ref[s * group : (s + 1) * group] = jnp.broadcast_to(column, (group, width))
        for k in range(chunks):
            cols = slice(k * LANES, (k + 1) * LANES)
            col_ref[k, :, s * LANES : (s + 1) * LANES] = jnp.broadcast_to(line[:, cols], (8, LANES))
    for k in range(chunks):
        cols = slice(k * LANES, (k + 1) * LANES)
        block_ref[k] = pick_ref[cols, cols]

    def lattice_chunk(k, carry):
        for c in range(channels):
            all_of(0, k, c).wait_recv()
            own_block(0, k, c).wait()

        def widen(at, carry):
            for c in range(channels):
                rows = pl.ds(pl.multiple_of(at * depth, depth), depth)
                block = recv_ref[k, c, at].astype(f32)
                for t in range(2):
                    wide_ref[c, t, rows] = block[:, t * LANES : (t + 1) * LANES]
            return carry

        lax.fori_loop(0, places, widen, 0)

        def row_step(i, carry):
            def lines(s):
                return pl.ds(s * group + i, count, stride=pair)

            blocks = [
                [
                    jnp.concatenate([wide_ref[c, t, lines(s)] for t in range(2)], axis=1).astype(bf16)
                    for s in range(2)
                ]
                for c in range(channels)
            ]
            for s in range(2):
                mixed = [None] * channels
                for c in range(channels):
                    own = dot(plus_ref[...], blocks[c][s])
                    crossed = dot(minus_ref[...], blocks[c][1 - s])
                    crossed = jnp.concatenate([crossed[:, LANES:], crossed[:, :LANES]], axis=1)
                    for d in range(channels):
                        term = own_ref[d, c] * own + cross_ref[d, c] * crossed
                        mixed[d] = term if c == 0 else mixed[d] + term
                reach = row_ref[pl.ds(s * group + i, 1)] + col_ref[k, :1]
                kept = cycle_ref[:, :width] <= reach
                for d in range(channels):
                    projected = jnp.where(kept, mixed[d] * (1.0 / count), 0.0).astype(bf16)
                    returned = dot(turn_ref[...], projected)
                    for t in range(2):
                        wide_ref[d, t, lines(s)] = returned[:, t * LANES : (t + 1) * LANES]
            return carry

        lax.fori_loop(0, group, row_step, 0)
        for c in range(channels):
            all_of(0, k, c).wait_send()

        def narrow(at, carry):
            for d in range(channels):
                rows = pl.ds(pl.multiple_of(at * depth, depth), depth)
                block = jnp.concatenate([wide_ref[d, t, rows] for t in range(2)], axis=1)
                send_ref[k, d, at] = block.astype(bf16)
            return carry

        lax.fori_loop(0, places, narrow, 0)
        for d in range(channels):
            backward(k, d)
        for d in range(channels):
            own_block(1, k, d).start()
        return carry

    lax.fori_loop(0, chunks, lattice_chunk, 0)

    def finish_unit(unit, carry):
        k, d = lax.div(unit, channels), lax.rem(unit, channels)
        all_of(1, k, d).wait_recv()
        own_block(1, k, d).wait()
        tiles = [
            base_ref.at[d, :, :, pl.ds(pl.multiple_of(k * LANES + t * half, LANES), LANES)] for t in range(2)
        ]
        arrivals = [pltpu.make_async_copy(back_ref.at[k, d], recv_ref.at[0, 0], finish_sem.at[2])] + [
            pltpu.make_async_copy(tiles[t], tile_buf.at[t], finish_sem.at[t]) for t in range(2)
        ]
        for copy in arrivals:
            copy.start()
        for copy in arrivals:
            copy.wait()

        def finish_matrix(n, carry):
            rows = pl.ds(pl.multiple_of(n * pair, pair), pair)
            block = recv_ref[0, 0, :, rows].astype(f32)
            for s in range(2):
                there = slice(s * half, (s + 1) * half)
                piece = block[:, s * group : (s + 1) * group].reshape(half, width)
                if s:
                    piece = dot(spread_ref[...], piece.astype(bf16))
                right = dot(piece[:, LANES:].astype(bf16), block_ref[k])
                for t, add in enumerate((piece[:, :LANES], right)):
                    tile_buf[t, n, there] = (tile_buf[t, n, there].astype(f32) + add).astype(bf16)
            return carry

        lax.fori_loop(0, mom_local, finish_matrix, 0)
        departures = [pltpu.make_async_copy(tile_buf.at[t], tiles[t], finish_sem.at[t]) for t in range(2)]
        for copy in departures:
            copy.start()
        for copy in departures:
            copy.wait()
        return carry

    units = chunks * channels
    lax.fori_loop(0, units - 1, finish_unit, 0)
    all_of(1, chunks - 1, channels - 1).wait_recv()
    own_block(1, chunks - 1, channels - 1).wait()

    def drain(unit, carry):
        all_of(1, lax.div(unit, channels), lax.rem(unit, channels)).wait_send()
        return carry

    lax.fori_loop(0, units, drain, 0)


def tile_finish_kernel(base_ref, received_ref, spread_ref, block_ref, out_ref):
    places, depth = received_ref.shape[2:4]
    batch, bonds = base_ref.shape[1:3]
    half = bonds // 2
    group = half // places
    pair = 2 * group

    def put(right):
        for n in range(batch):
            block = received_ref[0, 0, :, n * pair : (n + 1) * pair].astype(jnp.float32)
            for s in range(2):
                there = slice(s * half, (s + 1) * half)
                piece = block[:, s * group : (s + 1) * group].reshape(half, LANES)
                if s:
                    piece = dot(spread_ref[...], piece.astype(jnp.bfloat16))
                if right:
                    piece = dot(piece.astype(jnp.bfloat16), block_ref[...])
                out_ref[0, n, there] = (base_ref[0, n, there].astype(jnp.float32) + piece).astype(jnp.bfloat16)

    @pl.when(pl.program_id(0) == 0)
    def _():
        put(False)

    @pl.when(pl.program_id(0) == 1)
    def _():
        put(True)


def chunked_flow(vertex, loop_matrix, own_mix, cross_mix, shells, partner, grid_index):
    places = lax.axis_size("mom") * lax.axis_size("bond")
    channels, mom_local, bonds, _ = vertex.shape
    count = grid_index.shape[0]
    half = bonds // 2
    group = half // places
    chunks = half // LANES
    width = 2 * LANES
    depth = mom_local * 2 * group
    units = chunks * channels
    bf16, f32 = jnp.bfloat16, jnp.float32
    parts = mom_local // PAIR if mom_local % PAIR == 0 else 1
    anywhere = pl.BlockSpec(memory_space=pl.ANY)
    scalars = pl.BlockSpec(memory_space=pltpu.SMEM)
    inside = pl.BlockSpec(memory_space=pltpu.VMEM)
    dma = pltpu.SemaphoreType.DMA
    base, back = pl.pallas_call(
        functools.partial(flow_kernel, parts),
        in_specs=[anywhere, anywhere, scalars, scalars, inside, inside, inside],
        out_specs=[anywhere, anywhere],
        out_shape=[
            jax.ShapeDtypeStruct(vertex.shape, bf16),
            jax.ShapeDtypeStruct((chunks, channels, places, depth, width), bf16),
        ],
        scratch_shapes=[
            pltpu.VMEM((chunks, channels, places, depth, width), bf16),
            pltpu.VMEM((chunks, channels, places, depth, width), bf16),
            pltpu.VMEM((channels, 2, places * depth, LANES), f32),
            pltpu.VMEM((2, bonds, bonds), bf16),
            pltpu.VMEM((2, bonds, bonds), bf16),
            pltpu.VMEM((2, bonds, bonds), bf16),
            pltpu.VMEM((2, mom_local, bonds, LANES), bf16),
            pltpu.VMEM((half, half), bf16),
            pltpu.VMEM((half, half), bf16),
            pltpu.VMEM((chunks, LANES, LANES), bf16),
            pltpu.VMEM((count, count), bf16),
            pltpu.VMEM((count, count), bf16),
            pltpu.VMEM((count, count), bf16),
            pltpu.VMEM((count, count), f32),
            pltpu.VMEM((2 * group, width), f32),
            pltpu.VMEM((chunks, 8, width), f32),
            dma((2, 2)),
            dma((2,)),
            dma((units,)),
            dma((2, units)),
            dma((2, units)),
            dma((units,)),
            dma((3,)),
        ],
        compiler_params=pltpu.CompilerParams(collective_id=0, has_side_effects=True, vmem_limit_bytes=VMEM_LIMIT),
        name="flow",
    )(
        vertex,
        loop_matrix,
        own_mix,
        cross_mix,
        partner.reshape(1, bonds),
        shells.reshape(1, bonds),
        grid_index.reshape(1, count),
    )

    lower_partner = partner[:half] - half
    uppers = jnp.arange(half, dtype=jnp.int32)
    spread = (lower_partner[None, :] == uppers[:, None]).astype(bf16)
    edge = (chunks - 1) * LANES
    block = (lower_partner[edge:, None] - edge == uppers[None, :LANES]).astype(bf16)
    batch = math.gcd(mom_local, 4)
    tile = pl.BlockSpec((1, batch, bonds, LANES), lambda t, i: (channels - 1, i, 0, chunks - 1 + t * chunks))
    return pl.pallas_call(
        tile_finish_kernel,
        grid=(2, mom_local // batch),
        in_specs=[
            tile,
            pl.BlockSpec(
                (1, 1, places, batch * 2 * group, LANES), lambda t, i: (chunks - 1, channels - 1, 0, i, t)
            ),
            whole((half, half)),
            whole((LANES, LANES)),
        ],
        out_specs=tile,
        out_shape=jax.ShapeDtypeStruct(vertex.shape, bf16),
        input_output_aliases={0: 0},
        compiler_params=params(2),
        name="finish_tile",
    )(base, back, spread, block)


def per_device(vertex, *others):
    places = lax.axis_size("mom") * lax.axis_size("bond")
    half = vertex.shape[-1] // 2
    group = half // places
    if group and group % 8 == 0 and half % LANES == 0 and places * vertex.shape[1] >= 2 * LANES:
        return chunked_flow(vertex, *others)
    return general_flow(vertex, *others)


def solution(mesh):
    in_specs = (P(None, AXES, None, None), P(None, AXES, None, None), P(), P(), P(), P(), P())
    return jax.shard_map(
        per_device, mesh=mesh, in_specs=in_specs, out_specs=P(None, AXES, None, None), check_vma=False
    )
```

```python
import functools
import math

import jax
import jax.numpy as jnp
import numpy as np
from jax import lax
from jax.experimental import pallas as pl
from jax.experimental.layout import Layout, with_layout_constraint
from jax.experimental.pallas import tpu as pltpu
from jax.sharding import PartitionSpec as P

LANES = 128
PAIR = 2
ROWS = 2
VMEM_LIMIT = 58 * 1024 * 1024
AXES = ("mom", "bond")


def cas_table(grid_index, negate):
    count = grid_index.shape[0]
    side = math.isqrt(count)
    points = jnp.arange(count, dtype=jnp.int32)
    disp_x = points // side
    disp_y = points % side
    wave_x = grid_index // side
    wave_y = grid_index % side
    phases = (disp_x[:, None] * wave_x[None, :] + disp_y[:, None] * wave_y[None, :]) % side
    if negate:
        phases = (side - phases) % side
    angles = phases.astype(jnp.float32) * (2.0 * math.pi / side)
    return (jnp.cos(angles) + jnp.sin(angles)).astype(jnp.bfloat16)


def cycle_index(count):
    side = math.isqrt(count)
    points = jnp.arange(count, dtype=jnp.int32)
    centre_x = (points // side + side // 2) % side - side // 2
    centre_y = (points % side + side // 2) % side - side // 2
    return jnp.maximum(jnp.abs(centre_x), jnp.abs(centre_y))


def dot(a, b):
    return jnp.dot(a, b, preferred_element_type=jnp.float32)


def product_kernel(mom_local, places, vertex_ref, loop_ref, pick_ref, spread_ref, *refs):
    base_ref, send_ref, token_ref, wide_ref = refs[-4:]
    step = pl.program_id(1)
    token_ref[...] = jnp.zeros_like(token_ref)
    vertex = vertex_ref[0, 0]
    bonds = vertex.shape[0]
    half = bonds // 2
    group = half // places
    half_product = dot(vertex, loop_ref[0, 0]).astype(jnp.bfloat16)
    product = dot(half_product, vertex)
    base_ref[0, 0] = (product + vertex.astype(jnp.float32)).astype(jnp.bfloat16)
    rounded = product.astype(jnp.bfloat16)
    left = rounded[:, :half]
    right = dot(rounded[:, half:], spread_ref[...]).astype(jnp.bfloat16)
    for side, part in enumerate((left, right)):
        upper = dot(pick_ref[...], part[half:])
        lower = part[:half].astype(jnp.float32)
        for lane in range(half // LANES):
            at = side * (half // LANES) + lane
            cols = slice(lane * LANES, (lane + 1) * LANES)
            if mom_local == 1:
                wide_ref[at, :half] = lower[:, cols]
                wide_ref[at, half:] = upper[:, cols]
            else:
                wide_ref[at, pl.ds(step, half, stride=mom_local), :] = lower[:, cols]
                wide_ref[at, pl.ds(half * mom_local + step, half, stride=mom_local), :] = upper[:, cols]

    @pl.when(step == mom_local - 1)
    def _():
        for at in range(bonds // LANES):
            cols = slice(at * LANES, (at + 1) * LANES)
            for side in range(2):
                piece = wide_ref[at, side * half * mom_local : (side + 1) * half * mom_local]
                send_ref[:, 0, side, :, :, cols] = piece.reshape(places, group, mom_local, LANES).astype(jnp.bfloat16)


def first_product_kernel(places, vertex_ref, loop_ref, pick_ref, spread_ref, base_ref, send_ref, token_ref):
    token_ref[...] = jnp.zeros_like(token_ref)
    bonds = vertex_ref.shape[-1]
    half = bonds // 2
    group = half // places
    for n in range(vertex_ref.shape[1]):
        vertex = vertex_ref[0, n]
        half_product = dot(vertex, loop_ref[0, n]).astype(jnp.bfloat16)
        product = dot(half_product, vertex)
        base_ref[0, n] = (product + vertex.astype(jnp.float32)).astype(jnp.bfloat16)
        rounded = product.astype(jnp.bfloat16)
        left = rounded[:, :half]
        right = dot(rounded[:, half:], spread_ref[...]).astype(jnp.bfloat16)
        for side, part in enumerate((left, right)):
            cols = slice(side * half, (side + 1) * half)
            lower = part[:half].astype(jnp.float32)
            upper = dot(pick_ref[...], part[half:])
            send_ref[:, 0, n, 0, :, cols] = lower.reshape(places, group, half).astype(jnp.bfloat16)
            send_ref[:, 0, n, 1, :, cols] = upper.reshape(places, group, half).astype(jnp.bfloat16)


def lattice_kernel(sizes, targets, own_ref, cross_ref, plus_ref, minus_ref, back_ref, cycle_ref, reach_ref, *refs):
    received = [(refs[k], n) for k, size in enumerate(sizes) for n in range(size)]
    send_ref = refs[-1]
    places, _, _, _, mom_local, bonds = send_ref.shape
    count = places * mom_local
    half = bonds // 2
    for row in range(send_ref.shape[3]):
        blocks = [
            [
                ref[:, n, side, row].astype(jnp.float32).reshape(count, bonds).astype(jnp.bfloat16)
                for side in range(2)
            ]
            for ref, n in received
        ]
        for side in range(2):
            mixed = [None] * len(targets)
            for c in range(len(received)):
                own = dot(plus_ref[...], blocks[c][side])
                crossed = dot(minus_ref[...], blocks[c][1 - side])
                crossed = jnp.concatenate([crossed[:, half:], crossed[:, :half]], axis=1)
                for k, d in enumerate(targets):
                    term = own_ref[d, c] * own + cross_ref[d, c] * crossed
                    mixed[k] = term if c == 0 else mixed[k] + term
            kept = cycle_ref[...] <= reach_ref[side, row]
            for k in range(len(targets)):
                projected = jnp.where(kept, mixed[k], 0.0).astype(jnp.bfloat16)
                returned = dot(back_ref[...], projected)
                send_ref[:, k, side, row] = returned.reshape(places, mom_local, bonds).astype(jnp.bfloat16)


def finish_kernel(mom_local, base_ref, received_ref, pick_ref, spread_ref, out_ref, wide_ref):
    step = pl.program_id(1)
    places, _, _, group, _, bonds = received_ref.shape
    half = bonds // 2

    @pl.when(step == 0)
    def _():
        for at in range(bonds // LANES):
            cols = slice(at * LANES, (at + 1) * LANES)
            for side in range(2):
                piece = received_ref[:, 0, side, :, :, cols].astype(jnp.float32)
                wide_ref[at, side * half * mom_local : (side + 1) * half * mom_local] = piece.reshape(
                    half * mom_local, LANES
                )

    def rows_of(at):
        if mom_local == 1:
            return wide_ref[at]
        return wide_ref[at, pl.ds(step, bonds, stride=mom_local), :]

    tiles = half // LANES
    left = jnp.concatenate([rows_of(at) for at in range(tiles)], axis=1)
    right = jnp.concatenate([rows_of(at) for at in range(tiles, 2 * tiles)], axis=1)
    right = dot(right.astype(jnp.bfloat16), pick_ref[...])
    for side, part in enumerate((left, right)):
        cols = slice(side * half, (side + 1) * half)
        lower = part[:half]
        upper = dot(spread_ref[...], part[half:].astype(jnp.bfloat16))
        out_ref[0, 0, :half, cols] = (base_ref[0, 0, :half, cols].astype(jnp.float32) + lower).astype(jnp.bfloat16)
        out_ref[0, 0, half:, cols] = (base_ref[0, 0, half:, cols].astype(jnp.float32) + upper).astype(jnp.bfloat16)


def last_finish_kernel(base_ref, received_ref, pick_ref, spread_ref, out_ref):
    bonds = base_ref.shape[-1]
    half = bonds // 2
    for n in range(base_ref.shape[1]):
        for side in range(2):
            cols = slice(side * half, (side + 1) * half)
            lower = received_ref[:, 0, n, 0, :, cols].astype(jnp.float32).reshape(half, half)
            upper = received_ref[:, 0, n, 1, :, cols].astype(jnp.float32).reshape(half, half).astype(jnp.bfloat16)
            if side:
                lower = dot(lower.astype(jnp.bfloat16), pick_ref[...])
                upper = dot(upper, pick_ref[...]).astype(jnp.bfloat16)
            upper = dot(spread_ref[...], upper)
            out_ref[0, n, :half, cols] = (base_ref[0, n, :half, cols].astype(jnp.float32) + lower).astype(jnp.bfloat16)
            out_ref[0, n, half:, cols] = (base_ref[0, n, half:, cols].astype(jnp.float32) + upper).astype(jnp.bfloat16)


def whole(shape):
    return pl.BlockSpec(shape, lambda *steps: (0,) * len(shape))


def params(axes):
    return pltpu.CompilerParams(dimension_semantics=("arbitrary",) * axes, vmem_limit_bytes=VMEM_LIMIT)


def general_flow(vertex, loop_matrix, own_mix, cross_mix, shells, partner, grid_index):
    places = lax.axis_size("mom") * lax.axis_size("bond")
    place = lax.axis_index("mom") * lax.axis_size("bond") + lax.axis_index("bond")
    channels, mom_local, bonds, _ = vertex.shape
    count = grid_index.shape[0]
    half = bonds // 2
    group = half // places
    tiles = bonds // LANES
    bf16 = jnp.bfloat16
    first = list(range(channels))
    send_groups = [first[:1], first[1:]]
    back_groups = [first[:-1], first[-1:]]

    lower_partner = partner[:half] - half
    uppers = jnp.arange(half, dtype=jnp.int32)
    pick = (lower_partner[:, None] == uppers[None, :]).astype(bf16)
    spread = pick.T

    wide = pltpu.VMEM((tiles, bonds * mom_local, LANES), jnp.float32)
    square = (half, half)
    matmul = 2 * mom_local * bonds**3
    field_bytes = 2 * mom_local * bonds * bonds
    field = jax.ShapeDtypeStruct(vertex.shape, bf16)
    token_shape = jax.ShapeDtypeStruct((8, LANES), jnp.float32)

    def flow(members):
        return jax.ShapeDtypeStruct((places, members, 2, group, mom_local, bonds), bf16)

    def one_flow():
        return pl.BlockSpec((places, 1, 2, group, mom_local, bonds), lambda c, i: (0, c, 0, 0, 0, 0))

    def matrix_at(start):
        return pl.BlockSpec((1, 1, bonds, bonds), lambda c, i: (c + start, i, 0, 0))

    def exchange(outgoing):
        return lax.all_to_all(outgoing, AXES, split_axis=0, concat_axis=0, tiled=True)

    pair = PAIR if mom_local % PAIR == 0 else 1
    plain = jax.ShapeDtypeStruct((places, 1, mom_local, 2, group, bonds), bf16)
    plain_block = pl.BlockSpec((places, 1, pair, 2, group, bonds), lambda i: (0, 0, i, 0, 0, 0))

    def pair_at(start):
        return pl.BlockSpec((1, pair, bonds, bonds), lambda i: (start, i, 0, 0))

    base, outgoing, token = pl.pallas_call(
        functools.partial(first_product_kernel, places),
        grid=(mom_local // pair,),
        in_specs=[pair_at(0), pair_at(0), whole(square), whole(square)],
        out_specs=[pair_at(0), plain_block, whole(token_shape.shape)],
        out_shape=[field, plain, token_shape],
        compiler_params=params(1),
        cost_estimate=pl.CostEstimate(flops=5 * matmul // 2, bytes_accessed=4 * field_bytes, transcendentals=0),
        name="product_first",
    )(vertex, loop_matrix, pick, spread)
    whole_rows = with_layout_constraint(exchange(outgoing), Layout(major_to_minor=tuple(range(6))))
    arrived = [whole_rows.transpose(0, 1, 3, 4, 2, 5)]
    for members in send_groups[1:]:
        matrix = matrix_at(members[0])
        size = len(members)
        base, outgoing, _ = pl.pallas_call(
            functools.partial(product_kernel, mom_local, places),
            grid=(size, mom_local),
            in_specs=[matrix, matrix, whole(square), whole(square)]
            + [pl.BlockSpec(memory_space=pl.ANY)],
            out_specs=[matrix, one_flow(), whole(token_shape.shape)],
            out_shape=[field, flow(size), token_shape],
            input_output_aliases={4: 0},
            scratch_shapes=[wide],
            compiler_params=params(2),
            cost_estimate=pl.CostEstimate(
                flops=5 * size * matmul // 2, bytes_accessed=4 * size * field_bytes, transcendentals=0
            ),
            name="product_%d" % members[0],
        )(vertex, loop_matrix, pick, spread, base)
        arrived.append(exchange(outgoing))

    shells, partner, grid_index, own_mix, cross_mix, _ = lax.optimization_barrier(
        (shells, partner, grid_index, own_mix, cross_mix, token)
    )
    plus_table = cas_table(grid_index, False)
    minus_table = cas_table(grid_index, True)
    back_table = plus_table.T
    cycle = cycle_index(count)[:, None]
    shell_order = jnp.concatenate([shells[:half], jnp.take(shells, partner[:half])])
    shell_rows = lax.dynamic_slice_in_dim(shell_order.reshape(2, half), place * group, group, axis=1)
    reach = (shell_rows[:, :, None] + shell_order[None, None, :]).reshape(2, group, 1, bonds)
    own_scaled = own_mix * (1.0 / count)
    cross_scaled = cross_mix * (1.0 / count)

    rows = ROWS if group % ROWS == 0 else 1

    def row_block(members):
        return pl.BlockSpec((places, members, 2, rows, mom_local, bonds), lambda i: (0, 0, 0, i, 0, 0))

    table = whole((count, count))
    scalars = pl.BlockSpec(memory_space=pltpu.SMEM)
    sizes = [len(members) for members in send_groups]
    finished, earlier = [], []
    for members in back_groups:
        size = len(members)
        outgoing = pl.pallas_call(
            functools.partial(lattice_kernel, sizes, members),
            grid=(group // rows,),
            in_specs=[
                scalars,
                scalars,
                table,
                table,
                table,
                whole((count, 1)),
                pl.BlockSpec((2, rows, 1, bonds), lambda i: (0, i, 0, 0)),
            ]
            + [row_block(n) for n in sizes]
            + [pl.BlockSpec(memory_space=pl.ANY)] * len(earlier),
            out_specs=row_block(size),
            out_shape=flow(size),
            compiler_params=params(1),
            cost_estimate=pl.CostEstimate(
                flops=(2 * channels + size) * 2 * count * count * 2 * group * bonds,
                bytes_accessed=(channels + size) * field_bytes,
                transcendentals=0,
            ),
            name="lattice_%d" % members[0],
        )(own_scaled, cross_scaled, plus_table, minus_table, back_table, cycle, reach, *arrived, *earlier)
        earlier = [outgoing]
        if members is back_groups[-1]:
            outgoing = outgoing.transpose(0, 1, 4, 2, 3, 5)
        finished.append(exchange(outgoing))

    for members, received in zip(back_groups[:-1], finished[:-1]):
        matrix = matrix_at(members[0])
        size = len(members)
        base = pl.pallas_call(
            functools.partial(finish_kernel, mom_local),
            grid=(size, mom_local),
            in_specs=[matrix, one_flow(), whole(square), whole(square)],
            out_specs=matrix,
            out_shape=field,
            input_output_aliases={0: 0},
            scratch_shapes=[wide],
            compiler_params=params(2),
            cost_estimate=pl.CostEstimate(
                flops=size * matmul // 2, bytes_accessed=3 * size * field_bytes, transcendentals=0
            ),
            name="finish_%d" % members[0],
        )(base, received, pick, spread)
    last = back_groups[-1][0]
    return pl.pallas_call(
        last_finish_kernel,
        grid=(mom_local // pair,),
        in_specs=[pair_at(last), plain_block, whole(square), whole(square)],
        out_specs=pair_at(last),
        out_shape=field,
        input_output_aliases={0: 0},
        compiler_params=params(1),
        cost_estimate=pl.CostEstimate(flops=matmul // 2, bytes_accessed=3 * field_bytes, transcendentals=0),
        name="finish_last",
    )(base, finished[-1], pick, spread)


MESH = pl.DeviceIdType.MESH
FLOW_LIMIT = 44 * 1024 * 1024
LAST_LIMIT = 40 * 1024 * 1024


def flow_kernel(
    parts,
    vertex_ref,
    loop_ref,
    own_ref,
    cross_ref,
    partner_ref,
    shells_ref,
    grid_ref,
    base_ref,
    back_ref,
    send_ref,
    recv_ref,
    wide_ref,
    vertex_buf,
    loop_buf,
    pick_ref,
    spread_ref,
    block_ref,
    plus_ref,
    minus_ref,
    turn_ref,
    cycle_ref,
    row_ref,
    col_ref,
    load_sem,
    self_sem,
    out_sem,
    in_sem,
    home_sem,
    finish_sem,
):
    bf16, f32 = jnp.bfloat16, jnp.float32
    chunks, channels, places, depth, width = send_ref.shape
    mom_local, bonds = vertex_ref.shape[1], vertex_ref.shape[-1]
    half, count = bonds // 2, places * mom_local
    group = half // places
    pair = 2 * group
    side = math.isqrt(count)
    steps = channels * mom_local
    columns = lax.axis_size("bond")
    place = lax.axis_index("mom") * columns + lax.axis_index("bond")

    def device(offset):
        at = lax.rem(place + offset, places)
        return at, (lax.div(at, columns), lax.rem(at, columns))

    barrier = pltpu.get_barrier_semaphore()

    def greet(offset, carry):
        pl.semaphore_signal(barrier, inc=1, device_id=device(offset)[1], device_id_type=MESH)
        return carry

    lax.fori_loop(1, places, greet, 0)

    def loads(step, slot):
        c, n = lax.div(step, mom_local), lax.rem(step, mom_local)
        return [
            pltpu.make_async_copy(source.at[c, n], target.at[slot], load_sem.at[k, slot])
            for k, (source, target) in enumerate(((vertex_ref, vertex_buf), (loop_ref, loop_buf)))
        ]

    for copy in loads(0, 0):
        copy.start()

    down = lax.broadcasted_iota(jnp.int32, (half, half), 0)
    lower_partner = partner_ref[:, :half] - half
    pick_ref[...] = jnp.where(down == partner_ref[:, half:], 1.0, 0.0).astype(bf16)
    spread_ref[...] = jnp.where(down == lower_partner, 1.0, 0.0).astype(bf16)

    def forward(unit_k, unit_c, first, size):
        unit = unit_k * channels + unit_c

        def one(offset, carry):
            at, target = device(offset)
            rows = pl.ds(first, size)
            pltpu.make_async_remote_copy(
                src_ref=send_ref.at[unit_k, unit_c, at, rows],
                dst_ref=recv_ref.at[unit_k, unit_c, place, rows],
                send_sem=out_sem.at[0, unit],
                recv_sem=in_sem.at[0, unit],
                device_id=target,
                device_id_type=MESH,
            ).start()
            return carry

        lax.fori_loop(1, places, one, 0)

    def backward(unit_k, unit_c):
        unit = unit_k * channels + unit_c

        def one(offset, carry):
            at, target = device(offset)
            pltpu.make_async_remote_copy(
                src_ref=send_ref.at[unit_k, unit_c, at],
                dst_ref=back_ref.at[unit_k, unit_c, place],
                send_sem=out_sem.at[1, unit],
                recv_sem=in_sem.at[1, unit],
                device_id=target,
                device_id_type=MESH,
            ).start()
            return carry

        lax.fori_loop(1, places, one, 0)

    def all_of(way, unit_k, unit_c):
        unit = unit_k * channels + unit_c
        landing = back_ref if way else recv_ref
        return pltpu.make_async_remote_copy(
            src_ref=send_ref.at[unit_k, unit_c, pl.ds(0, places - 1)],
            dst_ref=landing.at[unit_k, unit_c, pl.ds(0, places - 1)],
            send_sem=out_sem.at[way, unit],
            recv_sem=in_sem.at[way, unit],
            device_id=device(1)[1],
            device_id_type=MESH,
        )

    def own_block(way, unit_k, unit_c):
        unit = unit_k * channels + unit_c
        landing, sem = (back_ref, home_sem) if way else (recv_ref, self_sem)
        return pltpu.make_async_copy(
            send_ref.at[unit_k, unit_c, place], landing.at[unit_k, unit_c, place], sem.at[unit]
        )

    part = mom_local // parts

    def product_step(step, carry):
        slot = lax.rem(step, 2)
        c, n = lax.div(step, mom_local), lax.rem(step, mom_local)

        @pl.when(step + 1 < steps)
        def _():
            for copy in loads(step + 1, 1 - slot):
                copy.start()

        for copy in loads(step, slot):
            copy.wait()
        vertex = vertex_buf[slot]
        half_product = dot(vertex, loop_buf[slot]).astype(bf16)
        product = dot(half_product, vertex)
        rounded = product.astype(bf16)
        left = rounded[:, :half]
        right = dot(rounded[:, half:], spread_ref[...]).astype(bf16)
        rows = pl.ds(pl.multiple_of(n * pair, pair), pair)
        for at, piece in enumerate((left, right)):
            upper = dot(pick_ref[...], piece[half:])
            lower = piece[:half].astype(f32)
            for k in range(chunks):
                cols = slice(k * LANES, (k + 1) * LANES)
                both = jnp.concatenate(
                    [lower[:, cols].reshape(places, group, LANES), upper[:, cols].reshape(places, group, LANES)], axis=1
                )
                send_ref[k, c, :, rows, at * LANES : (at + 1) * LANES] = both.astype(bf16)

        base_ref[c, n] = (product + vertex.astype(f32)).astype(bf16)

        @pl.when(step == part - 1)
        def _():
            pl.semaphore_wait(barrier, places - 1)

        @pl.when((c == 0) & (lax.rem(n, part) == part - 1))
        def _():
            forward(0, 0, pl.multiple_of((n - part + 1) * pair, part * pair), part * pair)

        @pl.when((c > 0) & (n == mom_local - 1))
        def _():
            forward(0, c, 0, depth)

        return carry

    lax.fori_loop(0, steps, product_step, 0)

    def later_chunk(unit, carry):
        forward(lax.div(unit, channels), lax.rem(unit, channels), 0, depth)
        return carry

    lax.fori_loop(channels, chunks * channels, later_chunk, 0)

    def start_own(unit, carry):
        own_block(0, lax.div(unit, channels), lax.rem(unit, channels)).start()
        return carry

    lax.fori_loop(0, chunks * channels, start_own, 0)

    def floor_div(value, by):
        return jnp.floor((value + 0.5) * (1.0 / by))

    points = lax.broadcasted_iota(jnp.int32, (count, count), 0).astype(f32)
    disp_x = floor_div(points, side)
    disp_y = points - side * disp_x
    far = []
    for disp in (disp_x, disp_y):
        moved = disp + side // 2
        far.append(jnp.abs(moved - side * floor_div(moved, side) - side // 2))
    cycle_ref[...] = jnp.maximum(far[0], far[1])
    grid = grid_ref[...].astype(f32)
    wave_x = floor_div(grid, side)
    wave_y = grid - side * wave_x
    phases = disp_x * wave_x + disp_y * wave_y
    phases = phases - side * floor_div(phases, side)
    angles = np.arange(side, dtype=np.float32) * np.float32(2.0 * math.pi / side)
    cas = (np.cos(angles) + np.sin(angles)).astype(np.float32)
    plus = jnp.zeros_like(phases)
    minus = jnp.zeros_like(phases)
    for phase in range(side):
        here = phases == float(phase)
        plus = jnp.where(here, float(cas[phase]), plus)
        minus = jnp.where(here, float(cas[(side - phase) % side]), minus)
    plus_ref[...] = plus.astype(bf16)
    minus_ref[...] = minus.astype(bf16)
    turn_ref[...] = plus.T.astype(bf16)

    shells = shells_ref[...].astype(f32)
    low_shells = shells[:, :half]
    up_shells = dot(jnp.broadcast_to(shells[:, half:], (8, half)).astype(bf16), spread_ref[...])[:1]
    lane = lax.broadcasted_iota(jnp.int32, (group, half), 1)
    mine = lane == place * group + lax.broadcasted_iota(jnp.int32, (group, half), 0)
    for s, line in enumerate((low_shells, up_shells)):
        column = jnp.sum(jnp.where(mine, jnp.broadcast_to(line, (group, half)), 0.0), axis=1, keepdims=True)
        row_ref[s * group : (s + 1) * group] = jnp.broadcast_to(column, (group, width))
        for k in range(chunks):
            cols = slice(k * LANES, (k + 1) * LANES)
            col_ref[k, :, s * LANES : (s + 1) * LANES] = jnp.broadcast_to(line[:, cols], (8, LANES))
    for k in range(chunks):
        cols = slice(k * LANES, (k + 1) * LANES)
        block_ref[k] = pick_ref[cols, cols]

    def lattice_chunk(k, carry):
        for c in range(channels):
            all_of(0, k, c).wait_recv()
            own_block(0, k, c).wait()

        def widen(at, carry):
            for c in range(channels):
                rows = pl.ds(pl.multiple_of(at * depth, depth), depth)
                block = recv_ref[k, c, at].astype(f32)
                for t in range(2):
                    wide_ref[c, t, rows] = block[:, t * LANES : (t + 1) * LANES]
            return carry

        lax.fori_loop(0, places, widen, 0)

        def row_step(i, carry):
            def lines(s):
                return pl.ds(s * group + i, count, stride=pair)

            blocks = [
                [
                    jnp.concatenate([wide_ref[c, t, lines(s)] for t in range(2)], axis=1).astype(bf16)
                    for s in range(2)
                ]
                for c in range(channels)
            ]
            for s in range(2):
                mixed = [None] * channels
                for c in range(channels):
                    own = dot(plus_ref[...], blocks[c][s])
                    crossed = dot(minus_ref[...], blocks[c][1 - s])
                    crossed = jnp.concatenate([crossed[:, LANES:], crossed[:, :LANES]], axis=1)
                    for d in range(channels):
                        term = own_ref[d, c] * own + cross_ref[d, c] * crossed
                        mixed[d] = term if c == 0 else mixed[d] + term
                reach = row_ref[pl.ds(s * group + i, 1)] + col_ref[k, :1]
                kept = cycle_ref[:, :width] <= reach
                for d in range(channels):
                    projected = jnp.where(kept, mixed[d] * (1.0 / count), 0.0).astype(bf16)
                    returned = dot(turn_ref[...], projected)
                    for t in range(2):
                        wide_ref[d, t, lines(s)] = returned[:, t * LANES : (t + 1) * LANES]
            return carry

        lax.fori_loop(0, group, row_step, 0)
        for c in range(channels):
            all_of(0, k, c).wait_send()

        def narrow(at, carry):
            for d in range(channels):
                rows = pl.ds(pl.multiple_of(at * depth, depth), depth)
                block = jnp.concatenate([wide_ref[d, t, rows] for t in range(2)], axis=1)
                send_ref[k, d, at] = block.astype(bf16)
            return carry

        lax.fori_loop(0, places, narrow, 0)
        for d in range(channels):
            backward(k, d)
        for d in range(channels):
            own_block(1, k, d).start()
        return carry

    lax.fori_loop(0, chunks, lattice_chunk, 0)

    def finish_unit(unit, carry):
        k, d = lax.div(unit, channels), lax.rem(unit, channels)
        all_of(1, k, d).wait_recv()
        own_block(1, k, d).wait()
        arrival = pltpu.make_async_copy(back_ref.at[k, d], recv_ref.at[0, 0], finish_sem)
        arrival.start()
        arrival.wait()

        def finish_matrix(n, carry):
            rows = pl.ds(pl.multiple_of(n * pair, pair), pair)
            block = recv_ref[0, 0, :, rows].astype(f32)
            for s in range(2):
                there = slice(s * half, (s + 1) * half)
                piece = block[:, s * group : (s + 1) * group].reshape(half, width)
                if s:
                    piece = dot(spread_ref[...], piece.astype(bf16))
                right = dot(piece[:, LANES:].astype(bf16), block_ref[k])
                for t, add in enumerate((piece[:, :LANES], right)):
                    cols = pl.ds(pl.multiple_of(k * LANES + t * half, LANES), LANES)
                    base_ref[d, n, there, cols] = (base_ref[d, n, there, cols].astype(f32) + add).astype(bf16)
            return carry

        lax.fori_loop(0, mom_local, finish_matrix, 0)
        return carry

    units = chunks * channels
    lax.fori_loop(0, units - 1, finish_unit, 0)
    all_of(1, chunks - 1, channels - 1).wait_recv()
    own_block(1, chunks - 1, channels - 1).wait()

    def drain(unit, carry):
        all_of(1, lax.div(unit, channels), lax.rem(unit, channels)).wait_send()
        return carry

    lax.fori_loop(0, units, drain, 0)


def last_kernel(base_ref, back_ref, partner_ref, out_ref, block_ref, tile_ref, in_sem, pass_sem, out_sem):
    bf16, f32 = jnp.bfloat16, jnp.float32
    chunks, channels, places, _, width = back_ref.shape
    mom_local, bonds = base_ref.shape[1:3]
    half = bonds // 2
    group = half // places
    pair = 2 * group
    d, edge = channels - 1, (chunks - 1) * LANES
    arrival = pltpu.make_async_copy(back_ref.at[chunks - 1, d], block_ref, in_sem)
    arrival.start()
    done = [(base_ref.at[c], out_ref.at[c]) for c in range(d)]
    for t in range(2):
        if edge:
            cols = pl.ds(t * half, edge)
            done.append((base_ref.at[d, :, :, cols], out_ref.at[d, :, :, cols]))
    passing = [pltpu.make_async_copy(*ends, pass_sem.at[at]) for at, ends in enumerate(done)]
    for copy in passing:
        copy.start()
    down = lax.broadcasted_iota(jnp.int32, (half, half), 0)
    spread = jnp.where(down == partner_ref[:, :half] - half, 1.0, 0.0).astype(bf16)
    pick = jnp.where(down[:LANES, :LANES] + edge == partner_ref[:, half + edge :], 1.0, 0.0).astype(bf16)
    arrival.wait()
    leaving = []
    for n in range(mom_local):
        block = block_ref[:, n * pair : (n + 1) * pair].astype(f32)
        for s in range(2):
            there = slice(s * half, (s + 1) * half)
            piece = block[:, s * group : (s + 1) * group].reshape(half, width)
            if s:
                piece = dot(spread, piece.astype(bf16))
            right = dot(piece[:, LANES:].astype(bf16), pick)
            for t, add in enumerate((piece[:, :LANES], right)):
                cols = slice(t * half + edge, t * half + edge + LANES)
                tile_ref[t, n, there] = (base_ref[d, n, there, cols].astype(f32) + add).astype(bf16)
        for t in range(2):
            cols = pl.ds(t * half + edge, LANES)
            copy = pltpu.make_async_copy(tile_ref.at[t, n], out_ref.at[d, n, :, cols], out_sem.at[t, n])
            copy.start()
            leaving.append(copy)
    for copy in passing + leaving:
        copy.wait()


def chunked_flow(vertex, loop_matrix, own_mix, cross_mix, shells, partner, grid_index):
    places = lax.axis_size("mom") * lax.axis_size("bond")
    channels, mom_local, bonds, _ = vertex.shape
    count = grid_index.shape[0]
    half = bonds // 2
    group = half // places
    chunks = half // LANES
    width = 2 * LANES
    depth = mom_local * 2 * group
    units = chunks * channels
    bf16, f32 = jnp.bfloat16, jnp.float32
    parts = mom_local // PAIR if mom_local % PAIR == 0 else 1
    anywhere = pl.BlockSpec(memory_space=pl.ANY)
    scalars = pl.BlockSpec(memory_space=pltpu.SMEM)
    inside = pl.BlockSpec(memory_space=pltpu.VMEM)
    dma = pltpu.SemaphoreType.DMA
    base, back = pl.pallas_call(
        functools.partial(flow_kernel, parts),
        in_specs=[anywhere, anywhere, scalars, scalars, inside, inside, inside],
        out_specs=[inside, anywhere],
        out_shape=[
            pltpu.VMEM(vertex.shape, bf16),
            pltpu.HBM((chunks, channels, places, depth, width), bf16),
        ],
        scratch_shapes=[
            pltpu.VMEM((chunks, channels, places, depth, width), bf16),
            pltpu.VMEM((chunks, channels, places, depth, width), bf16),
            pltpu.VMEM((channels, 2, places * depth, LANES), f32),
            pltpu.VMEM((2, bonds, bonds), bf16),
            pltpu.VMEM((2, bonds, bonds), bf16),
            pltpu.VMEM((half, half), bf16),
            pltpu.VMEM((half, half), bf16),
            pltpu.VMEM((chunks, LANES, LANES), bf16),
            pltpu.VMEM((count, count), bf16),
            pltpu.VMEM((count, count), bf16),
            pltpu.VMEM((count, count), bf16),
            pltpu.VMEM((count, count), f32),
            pltpu.VMEM((2 * group, width), f32),
            pltpu.VMEM((chunks, 8, width), f32),
            dma((2, 2)),
            dma((units,)),
            dma((2, units)),
            dma((2, units)),
            dma((units,)),
            dma(()),
        ],
        compiler_params=pltpu.CompilerParams(collective_id=0, has_side_effects=True, vmem_limit_bytes=FLOW_LIMIT),
        name="flow",
    )(
        vertex,
        loop_matrix,
        own_mix,
        cross_mix,
        partner.reshape(1, bonds),
        shells.reshape(1, bonds),
        grid_index.reshape(1, count),
    )

    return pl.pallas_call(
        last_kernel,
        in_specs=[inside, anywhere, inside],
        out_specs=anywhere,
        out_shape=pltpu.HBM(vertex.shape, bf16),
        scratch_shapes=[
            pltpu.VMEM((places, depth, width), bf16),
            pltpu.VMEM((2, mom_local, bonds, LANES), bf16),
            dma(()),
            dma((channels + 1,)),
            dma((2, mom_local)),
        ],
        compiler_params=pltpu.CompilerParams(vmem_limit_bytes=LAST_LIMIT),
        name="finish_last_unit",
    )(base, back, partner.reshape(1, bonds))


def per_device(vertex, *others):
    places = lax.axis_size("mom") * lax.axis_size("bond")
    half = vertex.shape[-1] // 2
    group = half // places
    if group and group % 8 == 0 and half % LANES == 0 and places * vertex.shape[1] >= 2 * LANES:
        return chunked_flow(vertex, *others)
    return general_flow(vertex, *others)


def solution(mesh):
    in_specs = (P(None, AXES, None, None), P(None, AXES, None, None), P(), P(), P(), P(), P())
    return jax.shard_map(
        per_device, mesh=mesh, in_specs=in_specs, out_specs=P(None, AXES, None, None), check_vma=False
    )
```

```python
import functools
import math

import jax
import jax.numpy as jnp
import numpy as np
from jax import lax
from jax.experimental import pallas as pl
from jax.experimental.layout import Layout, with_layout_constraint
from jax.experimental.pallas import tpu as pltpu
from jax.sharding import PartitionSpec as P

LANES = 128
PAIR = 2
ROWS = 2
VMEM_LIMIT = 58 * 1024 * 1024
AXES = ("mom", "bond")


def cas_table(grid_index, negate):
    count = grid_index.shape[0]
    side = math.isqrt(count)
    points = jnp.arange(count, dtype=jnp.int32)
    disp_x = points // side
    disp_y = points % side
    wave_x = grid_index // side
    wave_y = grid_index % side
    phases = (disp_x[:, None] * wave_x[None, :] + disp_y[:, None] * wave_y[None, :]) % side
    if negate:
        phases = (side - phases) % side
    angles = phases.astype(jnp.float32) * (2.0 * math.pi / side)
    return (jnp.cos(angles) + jnp.sin(angles)).astype(jnp.bfloat16)


def cycle_index(count):
    side = math.isqrt(count)
    points = jnp.arange(count, dtype=jnp.int32)
    centre_x = (points // side + side // 2) % side - side // 2
    centre_y = (points % side + side // 2) % side - side // 2
    return jnp.maximum(jnp.abs(centre_x), jnp.abs(centre_y))


def dot(a, b):
    return jnp.dot(a, b, preferred_element_type=jnp.float32)


def product_kernel(mom_local, places, vertex_ref, loop_ref, pick_ref, spread_ref, *refs):
    base_ref, send_ref, token_ref, wide_ref = refs[-4:]
    step = pl.program_id(1)
    token_ref[...] = jnp.zeros_like(token_ref)
    vertex = vertex_ref[0, 0]
    bonds = vertex.shape[0]
    half = bonds // 2
    group = half // places
    half_product = dot(vertex, loop_ref[0, 0]).astype(jnp.bfloat16)
    product = dot(half_product, vertex)
    base_ref[0, 0] = (product + vertex.astype(jnp.float32)).astype(jnp.bfloat16)
    rounded = product.astype(jnp.bfloat16)
    left = rounded[:, :half]
    right = dot(rounded[:, half:], spread_ref[...]).astype(jnp.bfloat16)
    for side, part in enumerate((left, right)):
        upper = dot(pick_ref[...], part[half:])
        lower = part[:half].astype(jnp.float32)
        for lane in range(half // LANES):
            at = side * (half // LANES) + lane
            cols = slice(lane * LANES, (lane + 1) * LANES)
            if mom_local == 1:
                wide_ref[at, :half] = lower[:, cols]
                wide_ref[at, half:] = upper[:, cols]
            else:
                wide_ref[at, pl.ds(step, half, stride=mom_local), :] = lower[:, cols]
                wide_ref[at, pl.ds(half * mom_local + step, half, stride=mom_local), :] = upper[:, cols]

    @pl.when(step == mom_local - 1)
    def _():
        for at in range(bonds // LANES):
            cols = slice(at * LANES, (at + 1) * LANES)
            for side in range(2):
                piece = wide_ref[at, side * half * mom_local : (side + 1) * half * mom_local]
                send_ref[:, 0, side, :, :, cols] = piece.reshape(places, group, mom_local, LANES).astype(jnp.bfloat16)


def first_product_kernel(places, vertex_ref, loop_ref, pick_ref, spread_ref, base_ref, send_ref, token_ref):
    token_ref[...] = jnp.zeros_like(token_ref)
    bonds = vertex_ref.shape[-1]
    half = bonds // 2
    group = half // places
    for n in range(vertex_ref.shape[1]):
        vertex = vertex_ref[0, n]
        half_product = dot(vertex, loop_ref[0, n]).astype(jnp.bfloat16)
        product = dot(half_product, vertex)
        base_ref[0, n] = (product + vertex.astype(jnp.float32)).astype(jnp.bfloat16)
        rounded = product.astype(jnp.bfloat16)
        left = rounded[:, :half]
        right = dot(rounded[:, half:], spread_ref[...]).astype(jnp.bfloat16)
        for side, part in enumerate((left, right)):
            cols = slice(side * half, (side + 1) * half)
            lower = part[:half].astype(jnp.float32)
            upper = dot(pick_ref[...], part[half:])
            send_ref[:, 0, n, 0, :, cols] = lower.reshape(places, group, half).astype(jnp.bfloat16)
            send_ref[:, 0, n, 1, :, cols] = upper.reshape(places, group, half).astype(jnp.bfloat16)


def lattice_kernel(sizes, targets, own_ref, cross_ref, plus_ref, minus_ref, back_ref, cycle_ref, reach_ref, *refs):
    received = [(refs[k], n) for k, size in enumerate(sizes) for n in range(size)]
    send_ref = refs[-1]
    places, _, _, _, mom_local, bonds = send_ref.shape
    count = places * mom_local
    half = bonds // 2
    for row in range(send_ref.shape[3]):
        blocks = [
            [
                ref[:, n, side, row].astype(jnp.float32).reshape(count, bonds).astype(jnp.bfloat16)
                for side in range(2)
            ]
            for ref, n in received
        ]
        for side in range(2):
            mixed = [None] * len(targets)
            for c in range(len(received)):
                own = dot(plus_ref[...], blocks[c][side])
                crossed = dot(minus_ref[...], blocks[c][1 - side])
                crossed = jnp.concatenate([crossed[:, half:], crossed[:, :half]], axis=1)
                for k, d in enumerate(targets):
                    term = own_ref[d, c] * own + cross_ref[d, c] * crossed
                    mixed[k] = term if c == 0 else mixed[k] + term
            kept = cycle_ref[...] <= reach_ref[side, row]
            for k in range(len(targets)):
                projected = jnp.where(kept, mixed[k], 0.0).astype(jnp.bfloat16)
                returned = dot(back_ref[...], projected)
                send_ref[:, k, side, row] = returned.reshape(places, mom_local, bonds).astype(jnp.bfloat16)


def finish_kernel(mom_local, base_ref, received_ref, pick_ref, spread_ref, out_ref, wide_ref):
    step = pl.program_id(1)
    places, _, _, group, _, bonds = received_ref.shape
    half = bonds // 2

    @pl.when(step == 0)
    def _():
        for at in range(bonds // LANES):
            cols = slice(at * LANES, (at + 1) * LANES)
            for side in range(2):
                piece = received_ref[:, 0, side, :, :, cols].astype(jnp.float32)
                wide_ref[at, side * half * mom_local : (side + 1) * half * mom_local] = piece.reshape(
                    half * mom_local, LANES
                )

    def rows_of(at):
        if mom_local == 1:
            return wide_ref[at]
        return wide_ref[at, pl.ds(step, bonds, stride=mom_local), :]

    tiles = half // LANES
    left = jnp.concatenate([rows_of(at) for at in range(tiles)], axis=1)
    right = jnp.concatenate([rows_of(at) for at in range(tiles, 2 * tiles)], axis=1)
    right = dot(right.astype(jnp.bfloat16), pick_ref[...])
    for side, part in enumerate((left, right)):
        cols = slice(side * half, (side + 1) * half)
        lower = part[:half]
        upper = dot(spread_ref[...], part[half:].astype(jnp.bfloat16))
        out_ref[0, 0, :half, cols] = (base_ref[0, 0, :half, cols].astype(jnp.float32) + lower).astype(jnp.bfloat16)
        out_ref[0, 0, half:, cols] = (base_ref[0, 0, half:, cols].astype(jnp.float32) + upper).astype(jnp.bfloat16)


def last_finish_kernel(base_ref, received_ref, pick_ref, spread_ref, out_ref):
    bonds = base_ref.shape[-1]
    half = bonds // 2
    for n in range(base_ref.shape[1]):
        for side in range(2):
            cols = slice(side * half, (side + 1) * half)
            lower = received_ref[:, 0, n, 0, :, cols].astype(jnp.float32).reshape(half, half)
            upper = received_ref[:, 0, n, 1, :, cols].astype(jnp.float32).reshape(half, half).astype(jnp.bfloat16)
            if side:
                lower = dot(lower.astype(jnp.bfloat16), pick_ref[...])
                upper = dot(upper, pick_ref[...]).astype(jnp.bfloat16)
            upper = dot(spread_ref[...], upper)
            out_ref[0, n, :half, cols] = (base_ref[0, n, :half, cols].astype(jnp.float32) + lower).astype(jnp.bfloat16)
            out_ref[0, n, half:, cols] = (base_ref[0, n, half:, cols].astype(jnp.float32) + upper).astype(jnp.bfloat16)


def whole(shape):
    return pl.BlockSpec(shape, lambda *steps: (0,) * len(shape))


def params(axes):
    return pltpu.CompilerParams(dimension_semantics=("arbitrary",) * axes, vmem_limit_bytes=VMEM_LIMIT)


def general_flow(vertex, loop_matrix, own_mix, cross_mix, shells, partner, grid_index):
    places = lax.axis_size("mom") * lax.axis_size("bond")
    place = lax.axis_index("mom") * lax.axis_size("bond") + lax.axis_index("bond")
    channels, mom_local, bonds, _ = vertex.shape
    count = grid_index.shape[0]
    half = bonds // 2
    group = half // places
    tiles = bonds // LANES
    bf16 = jnp.bfloat16
    first = list(range(channels))
    send_groups = [first[:1], first[1:]]
    back_groups = [first[:-1], first[-1:]]

    lower_partner = partner[:half] - half
    uppers = jnp.arange(half, dtype=jnp.int32)
    pick = (lower_partner[:, None] == uppers[None, :]).astype(bf16)
    spread = pick.T

    wide = pltpu.VMEM((tiles, bonds * mom_local, LANES), jnp.float32)
    square = (half, half)
    matmul = 2 * mom_local * bonds**3
    field_bytes = 2 * mom_local * bonds * bonds
    field = jax.ShapeDtypeStruct(vertex.shape, bf16)
    token_shape = jax.ShapeDtypeStruct((8, LANES), jnp.float32)

    def flow(members):
        return jax.ShapeDtypeStruct((places, members, 2, group, mom_local, bonds), bf16)

    def one_flow():
        return pl.BlockSpec((places, 1, 2, group, mom_local, bonds), lambda c, i: (0, c, 0, 0, 0, 0))

    def matrix_at(start):
        return pl.BlockSpec((1, 1, bonds, bonds), lambda c, i: (c + start, i, 0, 0))

    def exchange(outgoing):
        return lax.all_to_all(outgoing, AXES, split_axis=0, concat_axis=0, tiled=True)

    pair = PAIR if mom_local % PAIR == 0 else 1
    plain = jax.ShapeDtypeStruct((places, 1, mom_local, 2, group, bonds), bf16)
    plain_block = pl.BlockSpec((places, 1, pair, 2, group, bonds), lambda i: (0, 0, i, 0, 0, 0))

    def pair_at(start):
        return pl.BlockSpec((1, pair, bonds, bonds), lambda i: (start, i, 0, 0))

    base, outgoing, token = pl.pallas_call(
        functools.partial(first_product_kernel, places),
        grid=(mom_local // pair,),
        in_specs=[pair_at(0), pair_at(0), whole(square), whole(square)],
        out_specs=[pair_at(0), plain_block, whole(token_shape.shape)],
        out_shape=[field, plain, token_shape],
        compiler_params=params(1),
        cost_estimate=pl.CostEstimate(flops=5 * matmul // 2, bytes_accessed=4 * field_bytes, transcendentals=0),
        name="product_first",
    )(vertex, loop_matrix, pick, spread)
    whole_rows = with_layout_constraint(exchange(outgoing), Layout(major_to_minor=tuple(range(6))))
    arrived = [whole_rows.transpose(0, 1, 3, 4, 2, 5)]
    for members in send_groups[1:]:
        matrix = matrix_at(members[0])
        size = len(members)
        base, outgoing, _ = pl.pallas_call(
            functools.partial(product_kernel, mom_local, places),
            grid=(size, mom_local),
            in_specs=[matrix, matrix, whole(square), whole(square)]
            + [pl.BlockSpec(memory_space=pl.ANY)],
            out_specs=[matrix, one_flow(), whole(token_shape.shape)],
            out_shape=[field, flow(size), token_shape],
            input_output_aliases={4: 0},
            scratch_shapes=[wide],
            compiler_params=params(2),
            cost_estimate=pl.CostEstimate(
                flops=5 * size * matmul // 2, bytes_accessed=4 * size * field_bytes, transcendentals=0
            ),
            name="product_%d" % members[0],
        )(vertex, loop_matrix, pick, spread, base)
        arrived.append(exchange(outgoing))

    shells, partner, grid_index, own_mix, cross_mix, _ = lax.optimization_barrier(
        (shells, partner, grid_index, own_mix, cross_mix, token)
    )
    plus_table = cas_table(grid_index, False)
    minus_table = cas_table(grid_index, True)
    back_table = plus_table.T
    cycle = cycle_index(count)[:, None]
    shell_order = jnp.concatenate([shells[:half], jnp.take(shells, partner[:half])])
    shell_rows = lax.dynamic_slice_in_dim(shell_order.reshape(2, half), place * group, group, axis=1)
    reach = (shell_rows[:, :, None] + shell_order[None, None, :]).reshape(2, group, 1, bonds)
    own_scaled = own_mix * (1.0 / count)
    cross_scaled = cross_mix * (1.0 / count)

    rows = ROWS if group % ROWS == 0 else 1

    def row_block(members):
        return pl.BlockSpec((places, members, 2, rows, mom_local, bonds), lambda i: (0, 0, 0, i, 0, 0))

    table = whole((count, count))
    scalars = pl.BlockSpec(memory_space=pltpu.SMEM)
    sizes = [len(members) for members in send_groups]
    finished, earlier = [], []
    for members in back_groups:
        size = len(members)
        outgoing = pl.pallas_call(
            functools.partial(lattice_kernel, sizes, members),
            grid=(group // rows,),
            in_specs=[
                scalars,
                scalars,
                table,
                table,
                table,
                whole((count, 1)),
                pl.BlockSpec((2, rows, 1, bonds), lambda i: (0, i, 0, 0)),
            ]
            + [row_block(n) for n in sizes]
            + [pl.BlockSpec(memory_space=pl.ANY)] * len(earlier),
            out_specs=row_block(size),
            out_shape=flow(size),
            compiler_params=params(1),
            cost_estimate=pl.CostEstimate(
                flops=(2 * channels + size) * 2 * count * count * 2 * group * bonds,
                bytes_accessed=(channels + size) * field_bytes,
                transcendentals=0,
            ),
            name="lattice_%d" % members[0],
        )(own_scaled, cross_scaled, plus_table, minus_table, back_table, cycle, reach, *arrived, *earlier)
        earlier = [outgoing]
        if members is back_groups[-1]:
            outgoing = outgoing.transpose(0, 1, 4, 2, 3, 5)
        finished.append(exchange(outgoing))

    for members, received in zip(back_groups[:-1], finished[:-1]):
        matrix = matrix_at(members[0])
        size = len(members)
        base = pl.pallas_call(
            functools.partial(finish_kernel, mom_local),
            grid=(size, mom_local),
            in_specs=[matrix, one_flow(), whole(square), whole(square)],
            out_specs=matrix,
            out_shape=field,
            input_output_aliases={0: 0},
            scratch_shapes=[wide],
            compiler_params=params(2),
            cost_estimate=pl.CostEstimate(
                flops=size * matmul // 2, bytes_accessed=3 * size * field_bytes, transcendentals=0
            ),
            name="finish_%d" % members[0],
        )(base, received, pick, spread)
    last = back_groups[-1][0]
    return pl.pallas_call(
        last_finish_kernel,
        grid=(mom_local // pair,),
        in_specs=[pair_at(last), plain_block, whole(square), whole(square)],
        out_specs=pair_at(last),
        out_shape=field,
        input_output_aliases={0: 0},
        compiler_params=params(1),
        cost_estimate=pl.CostEstimate(flops=matmul // 2, bytes_accessed=3 * field_bytes, transcendentals=0),
        name="finish_last",
    )(base, finished[-1], pick, spread)


MESH = pl.DeviceIdType.MESH
FLOW_LIMIT = 44 * 1024 * 1024
LAST_LIMIT = 16 * 1024 * 1024


def flow_kernel(
    parts,
    vertex_ref,
    loop_ref,
    own_ref,
    cross_ref,
    partner_ref,
    shells_ref,
    grid_ref,
    base_ref,
    back_ref,
    tail_ref,
    send_ref,
    recv_ref,
    wide_ref,
    vertex_buf,
    loop_buf,
    pick_ref,
    spread_ref,
    block_ref,
    plus_ref,
    minus_ref,
    turn_ref,
    cycle_ref,
    row_ref,
    col_ref,
    load_sem,
    self_sem,
    out_sem,
    in_sem,
    home_sem,
    finish_sem,
):
    bf16, f32 = jnp.bfloat16, jnp.float32
    chunks, channels, places, depth, width = send_ref.shape
    mom_local, bonds = vertex_ref.shape[1], vertex_ref.shape[-1]
    half, count = bonds // 2, places * mom_local
    group = half // places
    pair = 2 * group
    side = math.isqrt(count)
    steps = channels * mom_local
    columns = lax.axis_size("bond")
    place = lax.axis_index("mom") * columns + lax.axis_index("bond")

    def device(offset):
        at = lax.rem(place + offset, places)
        return at, (lax.div(at, columns), lax.rem(at, columns))

    barrier = pltpu.get_barrier_semaphore()

    def greet(offset, carry):
        far = lax.rem(offset + places // 2 - 2, places - 1) + 1
        pl.semaphore_signal(barrier, inc=1, device_id=device(far)[1], device_id_type=MESH)
        return carry

    def loads(step, slot):
        c, n = lax.div(step, mom_local), lax.rem(step, mom_local)
        return [
            pltpu.make_async_copy(source.at[c, n], target.at[slot], load_sem.at[k, slot])
            for k, (source, target) in enumerate(((vertex_ref, vertex_buf), (loop_ref, loop_buf)))
        ]

    for copy in loads(0, 0):
        copy.start()
    lax.fori_loop(1, places, greet, 0)
    down = lax.broadcasted_iota(jnp.int32, (half, half), 0)
    lower_partner = partner_ref[:, :half] - half
    pick_ref[...] = jnp.where(down == partner_ref[:, half:], 1.0, 0.0).astype(bf16)
    spread_ref[...] = jnp.where(down == lower_partner, 1.0, 0.0).astype(bf16)

    def forward(unit_k, unit_c, first, size):
        unit = unit_k * channels + unit_c

        def one(offset, carry):
            at, target = device(offset)
            rows = pl.ds(first, size)
            pltpu.make_async_remote_copy(
                src_ref=send_ref.at[unit_k, unit_c, at, rows],
                dst_ref=recv_ref.at[unit_k, unit_c, place, rows],
                send_sem=out_sem.at[0, unit],
                recv_sem=in_sem.at[0, unit],
                device_id=target,
                device_id_type=MESH,
            ).start()
            return carry

        lax.fori_loop(1, places, one, 0)

    def backward(unit_k, unit_c, landing):
        unit = unit_k * channels + unit_c

        def one(offset, carry):
            at, target = device(offset)
            pltpu.make_async_remote_copy(
                src_ref=send_ref.at[unit_k, unit_c, at],
                dst_ref=landing.at[place],
                send_sem=out_sem.at[1, unit],
                recv_sem=in_sem.at[1, unit],
                device_id=target,
                device_id_type=MESH,
            ).start()
            return carry

        lax.fori_loop(1, places, one, 0)

    def landing_of(way, unit_k, unit_c):
        if way == 2:
            return tail_ref
        return (back_ref if way else recv_ref).at[unit_k, unit_c]

    def all_of(way, unit_k, unit_c):
        unit = unit_k * channels + unit_c
        return pltpu.make_async_remote_copy(
            src_ref=send_ref.at[unit_k, unit_c, pl.ds(0, places - 1)],
            dst_ref=landing_of(way, unit_k, unit_c).at[pl.ds(0, places - 1)],
            send_sem=out_sem.at[min(way, 1), unit],
            recv_sem=in_sem.at[min(way, 1), unit],
            device_id=device(1)[1],
            device_id_type=MESH,
        )

    def own_block(way, unit_k, unit_c):
        unit = unit_k * channels + unit_c
        return pltpu.make_async_copy(
            send_ref.at[unit_k, unit_c, place],
            landing_of(way, unit_k, unit_c).at[place],
            (home_sem if way else self_sem).at[unit],
        )

    part = mom_local // parts

    def product_step(step, carry):
        slot = lax.rem(step, 2)
        c, n = lax.div(step, mom_local), lax.rem(step, mom_local)

        @pl.when(step + 1 < steps)
        def _():
            for copy in loads(step + 1, 1 - slot):
                copy.start()

        for copy in loads(step, slot):
            copy.wait()
        vertex = vertex_buf[slot]
        half_product = dot(vertex, loop_buf[slot]).astype(bf16)
        product = dot(half_product, vertex)
        rounded = product.astype(bf16)
        left = rounded[:, :half]
        right = dot(rounded[:, half:], spread_ref[...]).astype(bf16)
        rows = pl.ds(pl.multiple_of(n * pair, pair), pair)
        for at, piece in enumerate((left, right)):
            upper = dot(pick_ref[...], piece[half:])
            lower = piece[:half].astype(f32)
            for k in range(chunks):
                cols = slice(k * LANES, (k + 1) * LANES)
                both = jnp.concatenate(
                    [lower[:, cols].reshape(places, group, LANES), upper[:, cols].reshape(places, group, LANES)], axis=1
                )
                send_ref[k, c, :, rows, at * LANES : (at + 1) * LANES] = both.astype(bf16)

        base_ref[c, n] = (product + vertex.astype(f32)).astype(bf16)

        @pl.when(step == part - 1)
        def _():
            pl.semaphore_wait(barrier, places - 1)

        @pl.when((c == 0) & (lax.rem(n, part) == part - 1))
        def _():
            forward(0, 0, pl.multiple_of((n - part + 1) * pair, part * pair), part * pair)

        @pl.when((c > 0) & (n == mom_local - 1))
        def _():
            forward(0, c, 0, depth)

        return carry

    lax.fori_loop(0, steps, product_step, 0)

    def later_chunk(unit, carry):
        forward(lax.div(unit, channels), lax.rem(unit, channels), 0, depth)
        return carry

    lax.fori_loop(channels, chunks * channels, later_chunk, 0)

    def start_own(unit, carry):
        own_block(0, lax.div(unit, channels), lax.rem(unit, channels)).start()
        return carry

    lax.fori_loop(0, chunks * channels, start_own, 0)

    def floor_div(value, by):
        return jnp.floor((value + 0.5) * (1.0 / by))

    points = lax.broadcasted_iota(jnp.int32, (count, count), 0).astype(f32)
    disp_x = floor_div(points, side)
    disp_y = points - side * disp_x
    far = []
    for disp in (disp_x, disp_y):
        moved = disp + side // 2
        far.append(jnp.abs(moved - side * floor_div(moved, side) - side // 2))
    cycle_ref[...] = jnp.maximum(far[0], far[1])
    grid = grid_ref[...].astype(f32)
    wave_x = floor_div(grid, side)
    wave_y = grid - side * wave_x
    phases = disp_x * wave_x + disp_y * wave_y
    phases = phases - side * floor_div(phases, side)
    angles = np.arange(side, dtype=np.float32) * np.float32(2.0 * math.pi / side)
    cas = (np.cos(angles) + np.sin(angles)).astype(np.float32)
    plus = jnp.zeros_like(phases)
    minus = jnp.zeros_like(phases)
    for phase in range(side):
        here = phases == float(phase)
        plus = jnp.where(here, float(cas[phase]), plus)
        minus = jnp.where(here, float(cas[(side - phase) % side]), minus)
    plus_ref[...] = plus.astype(bf16)
    minus_ref[...] = minus.astype(bf16)
    turn_ref[...] = plus.T.astype(bf16)

    shells = shells_ref[...].astype(f32)
    low_shells = shells[:, :half]
    up_shells = dot(jnp.broadcast_to(shells[:, half:], (8, half)).astype(bf16), spread_ref[...])[:1]
    lane = lax.broadcasted_iota(jnp.int32, (group, half), 1)
    mine = lane == place * group + lax.broadcasted_iota(jnp.int32, (group, half), 0)
    for s, line in enumerate((low_shells, up_shells)):
        column = jnp.sum(jnp.where(mine, jnp.broadcast_to(line, (group, half)), 0.0), axis=1, keepdims=True)
        row_ref[s * group : (s + 1) * group] = jnp.broadcast_to(column, (group, width))
        for k in range(chunks):
            cols = slice(k * LANES, (k + 1) * LANES)
            col_ref[k, :, s * LANES : (s + 1) * LANES] = jnp.broadcast_to(line[:, cols], (8, LANES))
    for k in range(chunks):
        cols = slice(k * LANES, (k + 1) * LANES)
        block_ref[k] = pick_ref[cols, cols]

    def lattice_chunk(k, carry):
        for c in range(channels):
            all_of(0, k, c).wait_recv()
            own_block(0, k, c).wait()

        def widen(at, carry):
            for c in range(channels):
                rows = pl.ds(pl.multiple_of(at * depth, depth), depth)
                block = recv_ref[k, c, at].astype(f32)
                for t in range(2):
                    wide_ref[c, t, rows] = block[:, t * LANES : (t + 1) * LANES]
            return carry

        lax.fori_loop(0, places, widen, 0)

        def row_step(i, carry):
            def lines(s):
                return pl.ds(s * group + i, count, stride=pair)

            blocks = [
                [
                    jnp.concatenate([wide_ref[c, t, lines(s)] for t in range(2)], axis=1).astype(bf16)
                    for s in range(2)
                ]
                for c in range(channels)
            ]
            for s in range(2):
                mixed = [None] * channels
                for c in range(channels):
                    own = dot(plus_ref[...], blocks[c][s])
                    crossed = dot(minus_ref[...], blocks[c][1 - s])
                    crossed = jnp.concatenate([crossed[:, LANES:], crossed[:, :LANES]], axis=1)
                    for d in range(channels):
                        term = own_ref[d, c] * own + cross_ref[d, c] * crossed
                        mixed[d] = term if c == 0 else mixed[d] + term
                reach = row_ref[pl.ds(s * group + i, 1)] + col_ref[k, :1]
                kept = cycle_ref[:, :width] <= reach
                for d in range(channels):
                    projected = jnp.where(kept, mixed[d] * (1.0 / count), 0.0).astype(bf16)
                    returned = dot(turn_ref[...], projected)
                    for t in range(2):
                        wide_ref[d, t, lines(s)] = returned[:, t * LANES : (t + 1) * LANES]
            return carry

        lax.fori_loop(0, group, row_step, 0)
        for c in range(channels):
            all_of(0, k, c).wait_send()

        def narrow(at, carry):
            for d in range(channels):
                rows = pl.ds(pl.multiple_of(at * depth, depth), depth)
                block = jnp.concatenate([wide_ref[d, t, rows] for t in range(2)], axis=1)
                send_ref[k, d, at] = block.astype(bf16)
            return carry

        lax.fori_loop(0, places, narrow, 0)
        for d in range(channels - 1):
            backward(k, d, back_ref.at[k, d])
            own_block(1, k, d).start()

        @pl.when(k < chunks - 1)
        def _():
            backward(k, channels - 1, back_ref.at[k, channels - 1])
            own_block(1, k, channels - 1).start()

        @pl.when(k == chunks - 1)
        def _():
            backward(k, channels - 1, tail_ref)
            own_block(2, k, channels - 1).start()

        return carry

    lax.fori_loop(0, chunks, lattice_chunk, 0)

    def finish_unit(unit, carry):
        k, d = lax.div(unit, channels), lax.rem(unit, channels)
        all_of(1, k, d).wait_recv()
        own_block(1, k, d).wait()
        arrival = pltpu.make_async_copy(back_ref.at[k, d], recv_ref.at[0, 0], finish_sem)
        arrival.start()
        arrival.wait()

        def finish_matrix(n, carry):
            rows = pl.ds(pl.multiple_of(n * pair, pair), pair)
            block = recv_ref[0, 0, :, rows].astype(f32)
            for s in range(2):
                there = slice(s * half, (s + 1) * half)
                piece = block[:, s * group : (s + 1) * group].reshape(half, width)
                if s:
                    piece = dot(spread_ref[...], piece.astype(bf16))
                right = dot(piece[:, LANES:].astype(bf16), block_ref[k])
                for t, add in enumerate((piece[:, :LANES], right)):
                    cols = pl.ds(pl.multiple_of(k * LANES + t * half, LANES), LANES)
                    base_ref[d, n, there, cols] = (base_ref[d, n, there, cols].astype(f32) + add).astype(bf16)
            return carry

        lax.fori_loop(0, mom_local, finish_matrix, 0)
        return carry

    units = chunks * channels
    lax.fori_loop(0, units - 1, finish_unit, 0)
    all_of(2, chunks - 1, channels - 1).wait_recv()
    own_block(2, chunks - 1, channels - 1).wait()

    def drain(unit, carry):
        all_of(1, lax.div(unit, channels), lax.rem(unit, channels)).wait_send()
        return carry

    lax.fori_loop(0, units, drain, 0)


def last_kernel(base_ref, block_ref, partner_ref, out_ref, tile_ref, pass_sem, out_sem):
    bf16, f32 = jnp.bfloat16, jnp.float32
    places, _, width = block_ref.shape
    channels, mom_local, bonds = base_ref.shape[:3]
    half = bonds // 2
    chunks = half // LANES
    group = half // places
    pair = 2 * group
    d, edge = channels - 1, (chunks - 1) * LANES
    done = [(base_ref.at[c], out_ref.at[c]) for c in range(d)]
    for t in range(2):
        if edge:
            cols = pl.ds(t * half, edge)
            done.append((base_ref.at[d, :, :, cols], out_ref.at[d, :, :, cols]))
    passing = [pltpu.make_async_copy(*ends, pass_sem.at[at]) for at, ends in enumerate(done)]
    for copy in passing:
        copy.start()
    down = lax.broadcasted_iota(jnp.int32, (half, half), 0)
    spread = jnp.where(down == partner_ref[:, :half] - half, 1.0, 0.0).astype(bf16)
    pick = jnp.where(down[:LANES, :LANES] + edge == partner_ref[:, half + edge :], 1.0, 0.0).astype(bf16)
    leaving = []
    for n in range(mom_local):
        block = block_ref[:, n * pair : (n + 1) * pair].astype(f32)
        for s in range(2):
            there = slice(s * half, (s + 1) * half)
            piece = block[:, s * group : (s + 1) * group].reshape(half, width)
            if s:
                piece = dot(spread, piece.astype(bf16))
            right = dot(piece[:, LANES:].astype(bf16), pick)
            for t, add in enumerate((piece[:, :LANES], right)):
                cols = slice(t * half + edge, t * half + edge + LANES)
                tile_ref[t, n, there] = (base_ref[d, n, there, cols].astype(f32) + add).astype(bf16)
        for t in range(2):
            cols = pl.ds(t * half + edge, LANES)
            copy = pltpu.make_async_copy(tile_ref.at[t, n], out_ref.at[d, n, :, cols], out_sem.at[t, n])
            copy.start()
            leaving.append(copy)
    for copy in passing + leaving:
        copy.wait()


def chunked_flow(vertex, loop_matrix, own_mix, cross_mix, shells, partner, grid_index):
    places = lax.axis_size("mom") * lax.axis_size("bond")
    channels, mom_local, bonds, _ = vertex.shape
    count = grid_index.shape[0]
    half = bonds // 2
    group = half // places
    chunks = half // LANES
    width = 2 * LANES
    depth = mom_local * 2 * group
    units = chunks * channels
    bf16, f32 = jnp.bfloat16, jnp.float32
    parts = mom_local // PAIR if mom_local % PAIR == 0 else 1
    anywhere = pl.BlockSpec(memory_space=pl.ANY)
    scalars = pl.BlockSpec(memory_space=pltpu.SMEM)
    inside = pl.BlockSpec(memory_space=pltpu.VMEM)
    dma = pltpu.SemaphoreType.DMA
    base, _, tail = pl.pallas_call(
        functools.partial(flow_kernel, parts),
        in_specs=[anywhere, anywhere, scalars, scalars, inside, inside, inside],
        out_specs=[inside, anywhere, inside],
        out_shape=[
            pltpu.VMEM(vertex.shape, bf16),
            pltpu.HBM((chunks, channels, places, depth, width), bf16),
            pltpu.VMEM((places, depth, width), bf16),
        ],
        scratch_shapes=[
            pltpu.VMEM((chunks, channels, places, depth, width), bf16),
            pltpu.VMEM((chunks, channels, places, depth, width), bf16),
            pltpu.VMEM((channels, 2, places * depth, LANES), f32),
            pltpu.VMEM((2, bonds, bonds), bf16),
            pltpu.VMEM((2, bonds, bonds), bf16),
            pltpu.VMEM((half, half), bf16),
            pltpu.VMEM((half, half), bf16),
            pltpu.VMEM((chunks, LANES, LANES), bf16),
            pltpu.VMEM((count, count), bf16),
            pltpu.VMEM((count, count), bf16),
            pltpu.VMEM((count, count), bf16),
            pltpu.VMEM((count, count), f32),
            pltpu.VMEM((2 * group, width), f32),
            pltpu.VMEM((chunks, 8, width), f32),
            dma((2, 2)),
            dma((units,)),
            dma((2, units)),
            dma((2, units)),
            dma((units,)),
            dma(()),
        ],
        compiler_params=pltpu.CompilerParams(collective_id=0, has_side_effects=True, vmem_limit_bytes=FLOW_LIMIT),
        name="flow",
    )(
        vertex,
        loop_matrix,
        own_mix,
        cross_mix,
        partner.reshape(1, bonds),
        shells.reshape(1, bonds),
        grid_index.reshape(1, count),
    )

    return pl.pallas_call(
        last_kernel,
        in_specs=[inside, inside, inside],
        out_specs=anywhere,
        out_shape=pltpu.HBM(vertex.shape, bf16),
        scratch_shapes=[
            pltpu.VMEM((2, mom_local, bonds, LANES), bf16),
            dma((channels + 1,)),
            dma((2, mom_local)),
        ],
        compiler_params=pltpu.CompilerParams(vmem_limit_bytes=LAST_LIMIT),
        name="finish_last_unit",
    )(base, tail, partner.reshape(1, bonds))


def per_device(vertex, *others):
    places = lax.axis_size("mom") * lax.axis_size("bond")
    half = vertex.shape[-1] // 2
    group = half // places
    if group and group % 8 == 0 and half % LANES == 0 and places * vertex.shape[1] >= 2 * LANES:
        return chunked_flow(vertex, *others)
    return general_flow(vertex, *others)


def solution(mesh):
    in_specs = (P(None, AXES, None, None), P(None, AXES, None, None), P(), P(), P(), P(), P())
    return jax.shard_map(
        per_device, mesh=mesh, in_specs=in_specs, out_specs=P(None, AXES, None, None), check_vma=False
    )
```

```python
import functools
import math

import jax
import jax.numpy as jnp
import numpy as np
from jax import lax
from jax.experimental import pallas as pl
from jax.experimental.layout import Layout, with_layout_constraint
from jax.experimental.pallas import tpu as pltpu
from jax.sharding import PartitionSpec as P

LANES = 128
PAIR = 2
ROWS = 2
VMEM_LIMIT = 58 * 1024 * 1024
AXES = ("mom", "bond")


def cas_table(grid_index, negate):
    count = grid_index.shape[0]
    side = math.isqrt(count)
    points = jnp.arange(count, dtype=jnp.int32)
    disp_x = points // side
    disp_y = points % side
    wave_x = grid_index // side
    wave_y = grid_index % side
    phases = (disp_x[:, None] * wave_x[None, :] + disp_y[:, None] * wave_y[None, :]) % side
    if negate:
        phases = (side - phases) % side
    angles = phases.astype(jnp.float32) * (2.0 * math.pi / side)
    return (jnp.cos(angles) + jnp.sin(angles)).astype(jnp.bfloat16)


def cycle_index(count):
    side = math.isqrt(count)
    points = jnp.arange(count, dtype=jnp.int32)
    centre_x = (points // side + side // 2) % side - side // 2
    centre_y = (points % side + side // 2) % side - side // 2
    return jnp.maximum(jnp.abs(centre_x), jnp.abs(centre_y))


def dot(a, b):
    return jnp.dot(a, b, preferred_element_type=jnp.float32)


def product_kernel(mom_local, places, vertex_ref, loop_ref, pick_ref, spread_ref, *refs):
    base_ref, send_ref, token_ref, wide_ref = refs[-4:]
    step = pl.program_id(1)
    token_ref[...] = jnp.zeros_like(token_ref)
    vertex = vertex_ref[0, 0]
    bonds = vertex.shape[0]
    half = bonds // 2
    group = half // places
    half_product = dot(vertex, loop_ref[0, 0]).astype(jnp.bfloat16)
    product = dot(half_product, vertex)
    base_ref[0, 0] = (product + vertex.astype(jnp.float32)).astype(jnp.bfloat16)
    rounded = product.astype(jnp.bfloat16)
    left = rounded[:, :half]
    right = dot(rounded[:, half:], spread_ref[...]).astype(jnp.bfloat16)
    for side, part in enumerate((left, right)):
        upper = dot(pick_ref[...], part[half:])
        lower = part[:half].astype(jnp.float32)
        for lane in range(half // LANES):
            at = side * (half // LANES) + lane
            cols = slice(lane * LANES, (lane + 1) * LANES)
            if mom_local == 1:
                wide_ref[at, :half] = lower[:, cols]
                wide_ref[at, half:] = upper[:, cols]
            else:
                wide_ref[at, pl.ds(step, half, stride=mom_local), :] = lower[:, cols]
                wide_ref[at, pl.ds(half * mom_local + step, half, stride=mom_local), :] = upper[:, cols]

    @pl.when(step == mom_local - 1)
    def _():
        for at in range(bonds // LANES):
            cols = slice(at * LANES, (at + 1) * LANES)
            for side in range(2):
                piece = wide_ref[at, side * half * mom_local : (side + 1) * half * mom_local]
                send_ref[:, 0, side, :, :, cols] = piece.reshape(places, group, mom_local, LANES).astype(jnp.bfloat16)


def first_product_kernel(places, vertex_ref, loop_ref, pick_ref, spread_ref, base_ref, send_ref, token_ref):
    token_ref[...] = jnp.zeros_like(token_ref)
    bonds = vertex_ref.shape[-1]
    half = bonds // 2
    group = half // places
    for n in range(vertex_ref.shape[1]):
        vertex = vertex_ref[0, n]
        half_product = dot(vertex, loop_ref[0, n]).astype(jnp.bfloat16)
        product = dot(half_product, vertex)
        base_ref[0, n] = (product + vertex.astype(jnp.float32)).astype(jnp.bfloat16)
        rounded = product.astype(jnp.bfloat16)
        left = rounded[:, :half]
        right = dot(rounded[:, half:], spread_ref[...]).astype(jnp.bfloat16)
        for side, part in enumerate((left, right)):
            cols = slice(side * half, (side + 1) * half)
            lower = part[:half].astype(jnp.float32)
            upper = dot(pick_ref[...], part[half:])
            send_ref[:, 0, n, 0, :, cols] = lower.reshape(places, group, half).astype(jnp.bfloat16)
            send_ref[:, 0, n, 1, :, cols] = upper.reshape(places, group, half).astype(jnp.bfloat16)


def lattice_kernel(sizes, targets, own_ref, cross_ref, plus_ref, minus_ref, back_ref, cycle_ref, reach_ref, *refs):
    received = [(refs[k], n) for k, size in enumerate(sizes) for n in range(size)]
    send_ref = refs[-1]
    places, _, _, _, mom_local, bonds = send_ref.shape
    count = places * mom_local
    half = bonds // 2
    for row in range(send_ref.shape[3]):
        blocks = [
            [
                ref[:, n, side, row].astype(jnp.float32).reshape(count, bonds).astype(jnp.bfloat16)
                for side in range(2)
            ]
            for ref, n in received
        ]
        for side in range(2):
            mixed = [None] * len(targets)
            for c in range(len(received)):
                own = dot(plus_ref[...], blocks[c][side])
                crossed = dot(minus_ref[...], blocks[c][1 - side])
                crossed = jnp.concatenate([crossed[:, half:], crossed[:, :half]], axis=1)
                for k, d in enumerate(targets):
                    term = own_ref[d, c] * own + cross_ref[d, c] * crossed
                    mixed[k] = term if c == 0 else mixed[k] + term
            kept = cycle_ref[...] <= reach_ref[side, row]
            for k in range(len(targets)):
                projected = jnp.where(kept, mixed[k], 0.0).astype(jnp.bfloat16)
                returned = dot(back_ref[...], projected)
                send_ref[:, k, side, row] = returned.reshape(places, mom_local, bonds).astype(jnp.bfloat16)


def finish_kernel(mom_local, base_ref, received_ref, pick_ref, spread_ref, out_ref, wide_ref):
    step = pl.program_id(1)
    places, _, _, group, _, bonds = received_ref.shape
    half = bonds // 2

    @pl.when(step == 0)
    def _():
        for at in range(bonds // LANES):
            cols = slice(at * LANES, (at + 1) * LANES)
            for side in range(2):
                piece = received_ref[:, 0, side, :, :, cols].astype(jnp.float32)
                wide_ref[at, side * half * mom_local : (side + 1) * half * mom_local] = piece.reshape(
                    half * mom_local, LANES
                )

    def rows_of(at):
        if mom_local == 1:
            return wide_ref[at]
        return wide_ref[at, pl.ds(step, bonds, stride=mom_local), :]

    tiles = half // LANES
    left = jnp.concatenate([rows_of(at) for at in range(tiles)], axis=1)
    right = jnp.concatenate([rows_of(at) for at in range(tiles, 2 * tiles)], axis=1)
    right = dot(right.astype(jnp.bfloat16), pick_ref[...])
    for side, part in enumerate((left, right)):
        cols = slice(side * half, (side + 1) * half)
        lower = part[:half]
        upper = dot(spread_ref[...], part[half:].astype(jnp.bfloat16))
        out_ref[0, 0, :half, cols] = (base_ref[0, 0, :half, cols].astype(jnp.float32) + lower).astype(jnp.bfloat16)
        out_ref[0, 0, half:, cols] = (base_ref[0, 0, half:, cols].astype(jnp.float32) + upper).astype(jnp.bfloat16)


def last_finish_kernel(base_ref, received_ref, pick_ref, spread_ref, out_ref):
    bonds = base_ref.shape[-1]
    half = bonds // 2
    for n in range(base_ref.shape[1]):
        for side in range(2):
            cols = slice(side * half, (side + 1) * half)
            lower = received_ref[:, 0, n, 0, :, cols].astype(jnp.float32).reshape(half, half)
            upper = received_ref[:, 0, n, 1, :, cols].astype(jnp.float32).reshape(half, half).astype(jnp.bfloat16)
            if side:
                lower = dot(lower.astype(jnp.bfloat16), pick_ref[...])
                upper = dot(upper, pick_ref[...]).astype(jnp.bfloat16)
            upper = dot(spread_ref[...], upper)
            out_ref[0, n, :half, cols] = (base_ref[0, n, :half, cols].astype(jnp.float32) + lower).astype(jnp.bfloat16)
            out_ref[0, n, half:, cols] = (base_ref[0, n, half:, cols].astype(jnp.float32) + upper).astype(jnp.bfloat16)


def whole(shape):
    return pl.BlockSpec(shape, lambda *steps: (0,) * len(shape))


def params(axes):
    return pltpu.CompilerParams(dimension_semantics=("arbitrary",) * axes, vmem_limit_bytes=VMEM_LIMIT)


def general_flow(vertex, loop_matrix, own_mix, cross_mix, shells, partner, grid_index):
    places = lax.axis_size("mom") * lax.axis_size("bond")
    place = lax.axis_index("mom") * lax.axis_size("bond") + lax.axis_index("bond")
    channels, mom_local, bonds, _ = vertex.shape
    count = grid_index.shape[0]
    half = bonds // 2
    group = half // places
    tiles = bonds // LANES
    bf16 = jnp.bfloat16
    first = list(range(channels))
    send_groups = [first[:1], first[1:]]
    back_groups = [first[:-1], first[-1:]]

    lower_partner = partner[:half] - half
    uppers = jnp.arange(half, dtype=jnp.int32)
    pick = (lower_partner[:, None] == uppers[None, :]).astype(bf16)
    spread = pick.T

    wide = pltpu.VMEM((tiles, bonds * mom_local, LANES), jnp.float32)
    square = (half, half)
    matmul = 2 * mom_local * bonds**3
    field_bytes = 2 * mom_local * bonds * bonds
    field = jax.ShapeDtypeStruct(vertex.shape, bf16)
    token_shape = jax.ShapeDtypeStruct((8, LANES), jnp.float32)

    def flow(members):
        return jax.ShapeDtypeStruct((places, members, 2, group, mom_local, bonds), bf16)

    def one_flow():
        return pl.BlockSpec((places, 1, 2, group, mom_local, bonds), lambda c, i: (0, c, 0, 0, 0, 0))

    def matrix_at(start):
        return pl.BlockSpec((1, 1, bonds, bonds), lambda c, i: (c + start, i, 0, 0))

    def exchange(outgoing):
        return lax.all_to_all(outgoing, AXES, split_axis=0, concat_axis=0, tiled=True)

    pair = PAIR if mom_local % PAIR == 0 else 1
    plain = jax.ShapeDtypeStruct((places, 1, mom_local, 2, group, bonds), bf16)
    plain_block = pl.BlockSpec((places, 1, pair, 2, group, bonds), lambda i: (0, 0, i, 0, 0, 0))

    def pair_at(start):
        return pl.BlockSpec((1, pair, bonds, bonds), lambda i: (start, i, 0, 0))

    base, outgoing, token = pl.pallas_call(
        functools.partial(first_product_kernel, places),
        grid=(mom_local // pair,),
        in_specs=[pair_at(0), pair_at(0), whole(square), whole(square)],
        out_specs=[pair_at(0), plain_block, whole(token_shape.shape)],
        out_shape=[field, plain, token_shape],
        compiler_params=params(1),
        cost_estimate=pl.CostEstimate(flops=5 * matmul // 2, bytes_accessed=4 * field_bytes, transcendentals=0),
        name="product_first",
    )(vertex, loop_matrix, pick, spread)
    whole_rows = with_layout_constraint(exchange(outgoing), Layout(major_to_minor=tuple(range(6))))
    arrived = [whole_rows.transpose(0, 1, 3, 4, 2, 5)]
    for members in send_groups[1:]:
        matrix = matrix_at(members[0])
        size = len(members)
        base, outgoing, _ = pl.pallas_call(
            functools.partial(product_kernel, mom_local, places),
            grid=(size, mom_local),
            in_specs=[matrix, matrix, whole(square), whole(square)]
            + [pl.BlockSpec(memory_space=pl.ANY)],
            out_specs=[matrix, one_flow(), whole(token_shape.shape)],
            out_shape=[field, flow(size), token_shape],
            input_output_aliases={4: 0},
            scratch_shapes=[wide],
            compiler_params=params(2),
            cost_estimate=pl.CostEstimate(
                flops=5 * size * matmul // 2, bytes_accessed=4 * size * field_bytes, transcendentals=0
            ),
            name="product_%d" % members[0],
        )(vertex, loop_matrix, pick, spread, base)
        arrived.append(exchange(outgoing))

    shells, partner, grid_index, own_mix, cross_mix, _ = lax.optimization_barrier(
        (shells, partner, grid_index, own_mix, cross_mix, token)
    )
    plus_table = cas_table(grid_index, False)
    minus_table = cas_table(grid_index, True)
    back_table = plus_table.T
    cycle = cycle_index(count)[:, None]
    shell_order = jnp.concatenate([shells[:half], jnp.take(shells, partner[:half])])
    shell_rows = lax.dynamic_slice_in_dim(shell_order.reshape(2, half), place * group, group, axis=1)
    reach = (shell_rows[:, :, None] + shell_order[None, None, :]).reshape(2, group, 1, bonds)
    own_scaled = own_mix * (1.0 / count)
    cross_scaled = cross_mix * (1.0 / count)

    rows = ROWS if group % ROWS == 0 else 1

    def row_block(members):
        return pl.BlockSpec((places, members, 2, rows, mom_local, bonds), lambda i: (0, 0, 0, i, 0, 0))

    table = whole((count, count))
    scalars = pl.BlockSpec(memory_space=pltpu.SMEM)
    sizes = [len(members) for members in send_groups]
    finished, earlier = [], []
    for members in back_groups:
        size = len(members)
        outgoing = pl.pallas_call(
            functools.partial(lattice_kernel, sizes, members),
            grid=(group // rows,),
            in_specs=[
                scalars,
                scalars,
                table,
                table,
                table,
                whole((count, 1)),
                pl.BlockSpec((2, rows, 1, bonds), lambda i: (0, i, 0, 0)),
            ]
            + [row_block(n) for n in sizes]
            + [pl.BlockSpec(memory_space=pl.ANY)] * len(earlier),
            out_specs=row_block(size),
            out_shape=flow(size),
            compiler_params=params(1),
            cost_estimate=pl.CostEstimate(
                flops=(2 * channels + size) * 2 * count * count * 2 * group * bonds,
                bytes_accessed=(channels + size) * field_bytes,
                transcendentals=0,
            ),
            name="lattice_%d" % members[0],
        )(own_scaled, cross_scaled, plus_table, minus_table, back_table, cycle, reach, *arrived, *earlier)
        earlier = [outgoing]
        if members is back_groups[-1]:
            outgoing = outgoing.transpose(0, 1, 4, 2, 3, 5)
        finished.append(exchange(outgoing))

    for members, received in zip(back_groups[:-1], finished[:-1]):
        matrix = matrix_at(members[0])
        size = len(members)
        base = pl.pallas_call(
            functools.partial(finish_kernel, mom_local),
            grid=(size, mom_local),
            in_specs=[matrix, one_flow(), whole(square), whole(square)],
            out_specs=matrix,
            out_shape=field,
            input_output_aliases={0: 0},
            scratch_shapes=[wide],
            compiler_params=params(2),
            cost_estimate=pl.CostEstimate(
                flops=size * matmul // 2, bytes_accessed=3 * size * field_bytes, transcendentals=0
            ),
            name="finish_%d" % members[0],
        )(base, received, pick, spread)
    last = back_groups[-1][0]
    return pl.pallas_call(
        last_finish_kernel,
        grid=(mom_local // pair,),
        in_specs=[pair_at(last), plain_block, whole(square), whole(square)],
        out_specs=pair_at(last),
        out_shape=field,
        input_output_aliases={0: 0},
        compiler_params=params(1),
        cost_estimate=pl.CostEstimate(flops=matmul // 2, bytes_accessed=3 * field_bytes, transcendentals=0),
        name="finish_last",
    )(base, finished[-1], pick, spread)


MESH = pl.DeviceIdType.MESH
FLOW_LIMIT = 44 * 1024 * 1024
LAST_LIMIT = 16 * 1024 * 1024


def flow_kernel(
    parts,
    vertex_ref,
    loop_ref,
    own_ref,
    cross_ref,
    partner_ref,
    shells_ref,
    grid_ref,
    base_ref,
    back_ref,
    tail_ref,
    send_ref,
    recv_ref,
    wide_ref,
    vertex_buf,
    loop_buf,
    pick_ref,
    spread_ref,
    block_ref,
    plus_ref,
    minus_ref,
    turn_ref,
    cycle_ref,
    row_ref,
    col_ref,
    load_sem,
    self_sem,
    out_sem,
    in_sem,
    home_sem,
    finish_sem,
):
    bf16, f32 = jnp.bfloat16, jnp.float32
    chunks, channels, places, depth, width = send_ref.shape
    mom_local, bonds = vertex_ref.shape[1], vertex_ref.shape[-1]
    half, count = bonds // 2, places * mom_local
    group = half // places
    pair = 2 * group
    side = math.isqrt(count)
    steps = channels * mom_local
    columns = lax.axis_size("bond")
    place = lax.axis_index("mom") * columns + lax.axis_index("bond")

    def device(offset):
        at = lax.rem(place + offset, places)
        return at, (lax.div(at, columns), lax.rem(at, columns))

    barrier = pltpu.get_barrier_semaphore()

    def greet(offset, carry):
        far = lax.rem(offset + places // 2 - 2, places - 1) + 1
        pl.semaphore_signal(barrier, inc=1, device_id=device(far)[1], device_id_type=MESH)
        return carry

    def loads(step, slot):
        c, n = lax.div(step, mom_local), lax.rem(step, mom_local)
        return [
            pltpu.make_async_copy(source.at[c, n], target.at[slot], load_sem.at[k, slot])
            for k, (source, target) in enumerate(((vertex_ref, vertex_buf), (loop_ref, loop_buf)))
        ]

    for copy in loads(0, 0):
        copy.start()
    lax.fori_loop(1, places, greet, 0)
    down = lax.broadcasted_iota(jnp.int32, (half, half), 0)
    lower_partner = partner_ref[:, :half] - half
    pick_ref[...] = jnp.where(down == partner_ref[:, half:], 1.0, 0.0).astype(bf16)
    spread_ref[...] = jnp.where(down == lower_partner, 1.0, 0.0).astype(bf16)

    def forward(unit_k, unit_c, first, size):
        unit = unit_k * channels + unit_c

        def one(offset, carry):
            at, target = device(offset)
            rows = pl.ds(first, size)
            pltpu.make_async_remote_copy(
                src_ref=send_ref.at[unit_k, unit_c, at, rows],
                dst_ref=recv_ref.at[unit_k, unit_c, place, rows],
                send_sem=out_sem.at[0, unit],
                recv_sem=in_sem.at[0, unit],
                device_id=target,
                device_id_type=MESH,
            ).start()
            return carry

        lax.fori_loop(1, places, one, 0)

    def backward(unit_k, unit_c, landing):
        unit = unit_k * channels + unit_c

        def one(offset, carry):
            at, target = device(offset)
            pltpu.make_async_remote_copy(
                src_ref=send_ref.at[unit_k, unit_c, at],
                dst_ref=landing.at[place],
                send_sem=out_sem.at[1, unit],
                recv_sem=in_sem.at[1, unit],
                device_id=target,
                device_id_type=MESH,
            ).start()
            return carry

        lax.fori_loop(1, places, one, 0)

    def landing_of(way, unit_k, unit_c):
        if way == 2:
            return tail_ref
        return (back_ref if way else recv_ref).at[unit_k, unit_c]

    def all_of(way, unit_k, unit_c):
        unit = unit_k * channels + unit_c
        return pltpu.make_async_remote_copy(
            src_ref=send_ref.at[unit_k, unit_c, pl.ds(0, places - 1)],
            dst_ref=landing_of(way, unit_k, unit_c).at[pl.ds(0, places - 1)],
            send_sem=out_sem.at[min(way, 1), unit],
            recv_sem=in_sem.at[min(way, 1), unit],
            device_id=device(1)[1],
            device_id_type=MESH,
        )

    def own_block(way, unit_k, unit_c):
        unit = unit_k * channels + unit_c
        return pltpu.make_async_copy(
            send_ref.at[unit_k, unit_c, place],
            landing_of(way, unit_k, unit_c).at[place],
            (home_sem if way else self_sem).at[unit],
        )

    part = mom_local // parts

    def product_step(step, carry):
        slot = lax.rem(step, 2)
        c, n = lax.div(step, mom_local), lax.rem(step, mom_local)

        @pl.when(step + 1 < steps)
        def _():
            for copy in loads(step + 1, 1 - slot):
                copy.start()

        for copy in loads(step, slot):
            copy.wait()
        vertex = vertex_buf[slot]
        half_product = dot(vertex, loop_buf[slot]).astype(bf16)
        product = dot(half_product, vertex)
        rounded = product.astype(bf16)
        left = rounded[:, :half]
        right = dot(rounded[:, half:], spread_ref[...]).astype(bf16)
        rows = pl.ds(pl.multiple_of(n * pair, pair), pair)
        for at, piece in enumerate((left, right)):
            upper = dot(pick_ref[...], piece[half:])
            lower = piece[:half].astype(f32)
            for k in range(chunks):
                cols = slice(k * LANES, (k + 1) * LANES)
                both = jnp.concatenate(
                    [lower[:, cols].reshape(places, group, LANES), upper[:, cols].reshape(places, group, LANES)], axis=1
                )
                send_ref[k, c, :, rows, at * LANES : (at + 1) * LANES] = both.astype(bf16)

        base_ref[c, n] = (product + vertex.astype(f32)).astype(bf16)

        @pl.when(step == part - 1)
        def _():
            pl.semaphore_wait(barrier, places - 1)

        @pl.when((c == 0) & (lax.rem(n, part) == part - 1))
        def _():
            forward(0, 0, pl.multiple_of((n - part + 1) * pair, part * pair), part * pair)

        @pl.when((c > 0) & (n == mom_local - 1))
        def _():
            forward(0, c, 0, depth)

        return carry

    lax.fori_loop(0, steps, product_step, 0)

    def later_chunk(unit, carry):
        forward(lax.div(unit, channels), lax.rem(unit, channels), 0, depth)
        return carry

    lax.fori_loop(channels, chunks * channels, later_chunk, 0)

    def start_own(unit, carry):
        own_block(0, lax.div(unit, channels), lax.rem(unit, channels)).start()
        return carry

    lax.fori_loop(0, chunks * channels, start_own, 0)

    def floor_div(value, by):
        return jnp.floor((value + 0.5) * (1.0 / by))

    points = lax.broadcasted_iota(jnp.int32, (count, count), 0).astype(f32)
    disp_x = floor_div(points, side)
    disp_y = points - side * disp_x
    far = []
    for disp in (disp_x, disp_y):
        moved = disp + side // 2
        far.append(jnp.abs(moved - side * floor_div(moved, side) - side // 2))
    cycle_ref[...] = jnp.maximum(far[0], far[1])
    grid = grid_ref[...].astype(f32)
    wave_x = floor_div(grid, side)
    wave_y = grid - side * wave_x
    phases = disp_x * wave_x + disp_y * wave_y
    phases = phases - side * floor_div(phases, side)
    angles = np.arange(side, dtype=np.float32) * np.float32(2.0 * math.pi / side)
    cas = (np.cos(angles) + np.sin(angles)).astype(np.float32)
    plus = jnp.zeros_like(phases)
    minus = jnp.zeros_like(phases)
    for phase in range(side):
        here = phases == float(phase)
        plus = jnp.where(here, float(cas[phase]), plus)
        minus = jnp.where(here, float(cas[(side - phase) % side]), minus)
    plus_ref[...] = plus.astype(bf16)
    minus_ref[...] = minus.astype(bf16)
    turn_ref[...] = plus.T.astype(bf16)

    shells = shells_ref[...].astype(f32)
    low_shells = shells[:, :half]
    up_shells = dot(jnp.broadcast_to(shells[:, half:], (8, half)).astype(bf16), spread_ref[...])[:1]
    lane = lax.broadcasted_iota(jnp.int32, (group, half), 1)
    mine = lane == place * group + lax.broadcasted_iota(jnp.int32, (group, half), 0)
    for s, line in enumerate((low_shells, up_shells)):
        column = jnp.sum(jnp.where(mine, jnp.broadcast_to(line, (group, half)), 0.0), axis=1, keepdims=True)
        row_ref[s * group : (s + 1) * group] = jnp.broadcast_to(column, (group, width))
        for k in range(chunks):
            cols = slice(k * LANES, (k + 1) * LANES)
            col_ref[k, :, s * LANES : (s + 1) * LANES] = jnp.broadcast_to(line[:, cols], (8, LANES))
    for k in range(chunks):
        cols = slice(k * LANES, (k + 1) * LANES)
        block_ref[k] = pick_ref[cols, cols]

    def lattice_chunk(k, carry):
        for c in range(channels):
            all_of(0, k, c).wait_recv()
            own_block(0, k, c).wait()

        def widen(at, carry):
            for c in range(channels):
                rows = pl.ds(pl.multiple_of(at * depth, depth), depth)
                block = recv_ref[k, c, at].astype(f32)
                for t in range(2):
                    wide_ref[c, t, rows] = block[:, t * LANES : (t + 1) * LANES]
            return carry

        lax.fori_loop(0, places, widen, 0)

        def row_step(i, carry):
            def lines(s):
                return pl.ds(s * group + i, count, stride=pair)

            blocks = [
                [
                    jnp.concatenate([wide_ref[c, t, lines(s)] for t in range(2)], axis=1).astype(bf16)
                    for s in range(2)
                ]
                for c in range(channels)
            ]
            for s in range(2):
                mixed = [None] * channels
                for c in range(channels):
                    own = dot(plus_ref[...], blocks[c][s])
                    crossed = dot(minus_ref[...], blocks[c][1 - s])
                    crossed = jnp.concatenate([crossed[:, LANES:], crossed[:, :LANES]], axis=1)
                    for d in range(channels):
                        term = own_ref[d, c] * own + cross_ref[d, c] * crossed
                        mixed[d] = term if c == 0 else mixed[d] + term
                reach = row_ref[pl.ds(s * group + i, 1)] + col_ref[k, :1]
                kept = cycle_ref[:, :width] <= reach
                for d in range(channels):
                    projected = jnp.where(kept, mixed[d] * (1.0 / count), 0.0).astype(bf16)
                    returned = dot(turn_ref[...], projected)
                    for t in range(2):
                        wide_ref[d, t, lines(s)] = returned[:, t * LANES : (t + 1) * LANES]
            return carry

        lax.fori_loop(0, group, row_step, 0)
        for c in range(channels):
            all_of(0, k, c).wait_send()

        def narrow(at, carry):
            for d in range(channels):
                rows = pl.ds(pl.multiple_of(at * depth, depth), depth)
                block = jnp.concatenate([wide_ref[d, t, rows] for t in range(2)], axis=1)
                send_ref[k, d, at] = block.astype(bf16)
            return carry

        lax.fori_loop(0, places, narrow, 0)
        for d in range(channels - 1):
            backward(k, d, back_ref.at[k, d])
            own_block(1, k, d).start()

        @pl.when(k < chunks - 1)
        def _():
            backward(k, channels - 1, back_ref.at[k, channels - 1])
            own_block(1, k, channels - 1).start()

        @pl.when(k == chunks - 1)
        def _():
            backward(k, channels - 1, tail_ref)
            own_block(2, k, channels - 1).start()

        return carry

    lax.fori_loop(0, chunks, lattice_chunk, 0)

    def finish_unit(unit, carry):
        k, d = lax.div(unit, channels), lax.rem(unit, channels)
        all_of(1, k, d).wait_recv()
        own_block(1, k, d).wait()
        arrival = pltpu.make_async_copy(back_ref.at[k, d], recv_ref.at[0, 0], finish_sem)
        arrival.start()
        arrival.wait()

        def finish_matrix(n, carry):
            rows = pl.ds(pl.multiple_of(n * pair, pair), pair)
            block = recv_ref[0, 0, :, rows].astype(f32)
            for s in range(2):
                there = slice(s * half, (s + 1) * half)
                piece = block[:, s * group : (s + 1) * group].reshape(half, width)
                if s:
                    piece = dot(spread_ref[...], piece.astype(bf16))
                right = dot(piece[:, LANES:].astype(bf16), block_ref[k])
                for t, add in enumerate((piece[:, :LANES], right)):
                    cols = pl.ds(pl.multiple_of(k * LANES + t * half, LANES), LANES)
                    base_ref[d, n, there, cols] = (base_ref[d, n, there, cols].astype(f32) + add).astype(bf16)
            return carry

        lax.fori_loop(0, mom_local, finish_matrix, 0)
        return carry

    units = chunks * channels
    lax.fori_loop(0, units - 1, finish_unit, 0)
    all_of(2, chunks - 1, channels - 1).wait_recv()
    own_block(2, chunks - 1, channels - 1).wait()

    def drain(unit, carry):
        all_of(1, lax.div(unit, channels), lax.rem(unit, channels)).wait_send()
        return carry

    lax.fori_loop(0, units, drain, 0)


def last_kernel(base_ref, block_ref, partner_ref, out_ref, tile_ref, pass_sem, out_sem):
    bf16, f32 = jnp.bfloat16, jnp.float32
    places, _, width = block_ref.shape
    channels, mom_local, bonds = base_ref.shape[:3]
    half = bonds // 2
    chunks = half // LANES
    group = half // places
    pair = 2 * group
    d, edge = channels - 1, (chunks - 1) * LANES
    done = [(base_ref.at[c], out_ref.at[c]) for c in range(d)]
    passing = [pltpu.make_async_copy(*ends, pass_sem.at[at]) for at, ends in enumerate(done)]
    for copy in passing:
        copy.start()
    down = lax.broadcasted_iota(jnp.int32, (half, half), 0)
    spread = jnp.where(down == partner_ref[:, :half] - half, 1.0, 0.0).astype(bf16)
    pick = jnp.where(down[:LANES, :LANES] + edge == partner_ref[:, half + edge :], 1.0, 0.0).astype(bf16)
    leaving = []
    for n in range(mom_local):
        block = block_ref[:, n * pair : (n + 1) * pair].astype(f32)
        for s in range(2):
            there = slice(s * half, (s + 1) * half)
            piece = block[:, s * group : (s + 1) * group].reshape(half, width)
            if s:
                piece = dot(spread, piece.astype(bf16))
            right = dot(piece[:, LANES:].astype(bf16), pick)
            for t, add in enumerate((piece[:, :LANES], right)):
                cols = slice(t * half + edge, t * half + edge + LANES)
                tile_ref[n, there, cols] = (base_ref[d, n, there, cols].astype(f32) + add).astype(bf16)
                if edge:
                    kept = slice(t * half, t * half + edge)
                    tile_ref[n, there, kept] = base_ref[d, n, there, kept]
        copy = pltpu.make_async_copy(tile_ref.at[n], out_ref.at[d, n], out_sem.at[n])
        copy.start()
        leaving.append(copy)
    for copy in passing + leaving:
        copy.wait()


def chunked_flow(vertex, loop_matrix, own_mix, cross_mix, shells, partner, grid_index):
    places = lax.axis_size("mom") * lax.axis_size("bond")
    channels, mom_local, bonds, _ = vertex.shape
    count = grid_index.shape[0]
    half = bonds // 2
    group = half // places
    chunks = half // LANES
    width = 2 * LANES
    depth = mom_local * 2 * group
    units = chunks * channels
    bf16, f32 = jnp.bfloat16, jnp.float32
    parts = mom_local // PAIR if mom_local % PAIR == 0 else 1
    anywhere = pl.BlockSpec(memory_space=pl.ANY)
    scalars = pl.BlockSpec(memory_space=pltpu.SMEM)
    inside = pl.BlockSpec(memory_space=pltpu.VMEM)
    dma = pltpu.SemaphoreType.DMA
    base, _, tail = pl.pallas_call(
        functools.partial(flow_kernel, parts),
        in_specs=[anywhere, anywhere, scalars, scalars, inside, inside, inside],
        out_specs=[inside, anywhere, inside],
        out_shape=[
            pltpu.VMEM(vertex.shape, bf16),
            pltpu.HBM((chunks, channels, places, depth, width), bf16),
            pltpu.VMEM((places, depth, width), bf16),
        ],
        scratch_shapes=[
            pltpu.VMEM((chunks, channels, places, depth, width), bf16),
            pltpu.VMEM((chunks, channels, places, depth, width), bf16),
            pltpu.VMEM((channels, 2, places * depth, LANES), f32),
            pltpu.VMEM((2, bonds, bonds), bf16),
            pltpu.VMEM((2, bonds, bonds), bf16),
            pltpu.VMEM((half, half), bf16),
            pltpu.VMEM((half, half), bf16),
            pltpu.VMEM((chunks, LANES, LANES), bf16),
            pltpu.VMEM((count, count), bf16),
            pltpu.VMEM((count, count), bf16),
            pltpu.VMEM((count, count), bf16),
            pltpu.VMEM((count, count), f32),
            pltpu.VMEM((2 * group, width), f32),
            pltpu.VMEM((chunks, 8, width), f32),
            dma((2, 2)),
            dma((units,)),
            dma((2, units)),
            dma((2, units)),
            dma((units,)),
            dma(()),
        ],
        compiler_params=pltpu.CompilerParams(collective_id=0, has_side_effects=True, vmem_limit_bytes=FLOW_LIMIT),
        name="flow",
    )(
        vertex,
        loop_matrix,
        own_mix,
        cross_mix,
        partner.reshape(1, bonds),
        shells.reshape(1, bonds),
        grid_index.reshape(1, count),
    )

    return pl.pallas_call(
        last_kernel,
        in_specs=[inside, inside, inside],
        out_specs=anywhere,
        out_shape=pltpu.HBM(vertex.shape, bf16),
        scratch_shapes=[
            pltpu.VMEM((mom_local, bonds, bonds), bf16),
            dma((channels,)),
            dma((mom_local,)),
        ],
        compiler_params=pltpu.CompilerParams(vmem_limit_bytes=LAST_LIMIT),
        name="finish_last_unit",
    )(base, tail, partner.reshape(1, bonds))


def per_device(vertex, *others):
    places = lax.axis_size("mom") * lax.axis_size("bond")
    half = vertex.shape[-1] // 2
    group = half // places
    if group and group % 8 == 0 and half % LANES == 0 and places * vertex.shape[1] >= 2 * LANES:
        return chunked_flow(vertex, *others)
    return general_flow(vertex, *others)


def solution(mesh):
    in_specs = (P(None, AXES, None, None), P(None, AXES, None, None), P(), P(), P(), P(), P())
    return jax.shard_map(
        per_device, mesh=mesh, in_specs=in_specs, out_specs=P(None, AXES, None, None), check_vma=False
    )
```

```python
import functools
import math

import jax
import jax.numpy as jnp
import numpy as np
from jax import lax
from jax.experimental import pallas as pl
from jax.experimental.layout import Layout, with_layout_constraint
from jax.experimental.pallas import tpu as pltpu
from jax.sharding import PartitionSpec as P

LANES = 128
PAIR = 2
ROWS = 2
VMEM_LIMIT = 58 * 1024 * 1024
AXES = ("mom", "bond")


def cas_table(grid_index, negate):
    count = grid_index.shape[0]
    side = math.isqrt(count)
    points = jnp.arange(count, dtype=jnp.int32)
    disp_x = points // side
    disp_y = points % side
    wave_x = grid_index // side
    wave_y = grid_index % side
    phases = (disp_x[:, None] * wave_x[None, :] + disp_y[:, None] * wave_y[None, :]) % side
    if negate:
        phases = (side - phases) % side
    angles = phases.astype(jnp.float32) * (2.0 * math.pi / side)
    return (jnp.cos(angles) + jnp.sin(angles)).astype(jnp.bfloat16)


def cycle_index(count):
    side = math.isqrt(count)
    points = jnp.arange(count, dtype=jnp.int32)
    centre_x = (points // side + side // 2) % side - side // 2
    centre_y = (points % side + side // 2) % side - side // 2
    return jnp.maximum(jnp.abs(centre_x), jnp.abs(centre_y))


def dot(a, b):
    return jnp.dot(a, b, preferred_element_type=jnp.float32)


def product_kernel(mom_local, places, vertex_ref, loop_ref, pick_ref, spread_ref, *refs):
    base_ref, send_ref, token_ref, wide_ref = refs[-4:]
    step = pl.program_id(1)
    token_ref[...] = jnp.zeros_like(token_ref)
    vertex = vertex_ref[0, 0]
    bonds = vertex.shape[0]
    half = bonds // 2
    group = half // places
    half_product = dot(vertex, loop_ref[0, 0]).astype(jnp.bfloat16)
    product = dot(half_product, vertex)
    base_ref[0, 0] = (product + vertex.astype(jnp.float32)).astype(jnp.bfloat16)
    rounded = product.astype(jnp.bfloat16)
    left = rounded[:, :half]
    right = dot(rounded[:, half:], spread_ref[...]).astype(jnp.bfloat16)
    for side, part in enumerate((left, right)):
        upper = dot(pick_ref[...], part[half:])
        lower = part[:half].astype(jnp.float32)
        for lane in range(half // LANES):
            at = side * (half // LANES) + lane
            cols = slice(lane * LANES, (lane + 1) * LANES)
            if mom_local == 1:
                wide_ref[at, :half] = lower[:, cols]
                wide_ref[at, half:] = upper[:, cols]
            else:
                wide_ref[at, pl.ds(step, half, stride=mom_local), :] = lower[:, cols]
                wide_ref[at, pl.ds(half * mom_local + step, half, stride=mom_local), :] = upper[:, cols]

    @pl.when(step == mom_local - 1)
    def _():
        for at in range(bonds // LANES):
            cols = slice(at * LANES, (at + 1) * LANES)
            for side in range(2):
                piece = wide_ref[at, side * half * mom_local : (side + 1) * half * mom_local]
                send_ref[:, 0, side, :, :, cols] = piece.reshape(places, group, mom_local, LANES).astype(jnp.bfloat16)


def first_product_kernel(places, vertex_ref, loop_ref, pick_ref, spread_ref, base_ref, send_ref, token_ref):
    token_ref[...] = jnp.zeros_like(token_ref)
    bonds = vertex_ref.shape[-1]
    half = bonds // 2
    group = half // places
    for n in range(vertex_ref.shape[1]):
        vertex = vertex_ref[0, n]
        half_product = dot(vertex, loop_ref[0, n]).astype(jnp.bfloat16)
        product = dot(half_product, vertex)
        base_ref[0, n] = (product + vertex.astype(jnp.float32)).astype(jnp.bfloat16)
        rounded = product.astype(jnp.bfloat16)
        left = rounded[:, :half]
        right = dot(rounded[:, half:], spread_ref[...]).astype(jnp.bfloat16)
        for side, part in enumerate((left, right)):
            cols = slice(side * half, (side + 1) * half)
            lower = part[:half].astype(jnp.float32)
            upper = dot(pick_ref[...], part[half:])
            send_ref[:, 0, n, 0, :, cols] = lower.reshape(places, group, half).astype(jnp.bfloat16)
            send_ref[:, 0, n, 1, :, cols] = upper.reshape(places, group, half).astype(jnp.bfloat16)


def lattice_kernel(sizes, targets, own_ref, cross_ref, plus_ref, minus_ref, back_ref, cycle_ref, reach_ref, *refs):
    received = [(refs[k], n) for k, size in enumerate(sizes) for n in range(size)]
    send_ref = refs[-1]
    places, _, _, _, mom_local, bonds = send_ref.shape
    count = places * mom_local
    half = bonds // 2
    for row in range(send_ref.shape[3]):
        blocks = [
            [
                ref[:, n, side, row].astype(jnp.float32).reshape(count, bonds).astype(jnp.bfloat16)
                for side in range(2)
            ]
            for ref, n in received
        ]
        for side in range(2):
            mixed = [None] * len(targets)
            for c in range(len(received)):
                own = dot(plus_ref[...], blocks[c][side])
                crossed = dot(minus_ref[...], blocks[c][1 - side])
                crossed = jnp.concatenate([crossed[:, half:], crossed[:, :half]], axis=1)
                for k, d in enumerate(targets):
                    term = own_ref[d, c] * own + cross_ref[d, c] * crossed
                    mixed[k] = term if c == 0 else mixed[k] + term
            kept = cycle_ref[...] <= reach_ref[side, row]
            for k in range(len(targets)):
                projected = jnp.where(kept, mixed[k], 0.0).astype(jnp.bfloat16)
                returned = dot(back_ref[...], projected)
                send_ref[:, k, side, row] = returned.reshape(places, mom_local, bonds).astype(jnp.bfloat16)


def finish_kernel(mom_local, base_ref, received_ref, pick_ref, spread_ref, out_ref, wide_ref):
    step = pl.program_id(1)
    places, _, _, group, _, bonds = received_ref.shape
    half = bonds // 2

    @pl.when(step == 0)
    def _():
        for at in range(bonds // LANES):
            cols = slice(at * LANES, (at + 1) * LANES)
            for side in range(2):
                piece = received_ref[:, 0, side, :, :, cols].astype(jnp.float32)
                wide_ref[at, side * half * mom_local : (side + 1) * half * mom_local] = piece.reshape(
                    half * mom_local, LANES
                )

    def rows_of(at):
        if mom_local == 1:
            return wide_ref[at]
        return wide_ref[at, pl.ds(step, bonds, stride=mom_local), :]

    tiles = half // LANES
    left = jnp.concatenate([rows_of(at) for at in range(tiles)], axis=1)
    right = jnp.concatenate([rows_of(at) for at in range(tiles, 2 * tiles)], axis=1)
    right = dot(right.astype(jnp.bfloat16), pick_ref[...])
    for side, part in enumerate((left, right)):
        cols = slice(side * half, (side + 1) * half)
        lower = part[:half]
        upper = dot(spread_ref[...], part[half:].astype(jnp.bfloat16))
        out_ref[0, 0, :half, cols] = (base_ref[0, 0, :half, cols].astype(jnp.float32) + lower).astype(jnp.bfloat16)
        out_ref[0, 0, half:, cols] = (base_ref[0, 0, half:, cols].astype(jnp.float32) + upper).astype(jnp.bfloat16)


def last_finish_kernel(base_ref, received_ref, pick_ref, spread_ref, out_ref):
    bonds = base_ref.shape[-1]
    half = bonds // 2
    for n in range(base_ref.shape[1]):
        for side in range(2):
            cols = slice(side * half, (side + 1) * half)
            lower = received_ref[:, 0, n, 0, :, cols].astype(jnp.float32).reshape(half, half)
            upper = received_ref[:, 0, n, 1, :, cols].astype(jnp.float32).reshape(half, half).astype(jnp.bfloat16)
            if side:
                lower = dot(lower.astype(jnp.bfloat16), pick_ref[...])
                upper = dot(upper, pick_ref[...]).astype(jnp.bfloat16)
            upper = dot(spread_ref[...], upper)
            out_ref[0, n, :half, cols] = (base_ref[0, n, :half, cols].astype(jnp.float32) + lower).astype(jnp.bfloat16)
            out_ref[0, n, half:, cols] = (base_ref[0, n, half:, cols].astype(jnp.float32) + upper).astype(jnp.bfloat16)


def whole(shape):
    return pl.BlockSpec(shape, lambda *steps: (0,) * len(shape))


def params(axes):
    return pltpu.CompilerParams(dimension_semantics=("arbitrary",) * axes, vmem_limit_bytes=VMEM_LIMIT)


def general_flow(vertex, loop_matrix, own_mix, cross_mix, shells, partner, grid_index):
    places = lax.axis_size("mom") * lax.axis_size("bond")
    place = lax.axis_index("mom") * lax.axis_size("bond") + lax.axis_index("bond")
    channels, mom_local, bonds, _ = vertex.shape
    count = grid_index.shape[0]
    half = bonds // 2
    group = half // places
    tiles = bonds // LANES
    bf16 = jnp.bfloat16
    first = list(range(channels))
    send_groups = [first[:1], first[1:]]
    back_groups = [first[:-1], first[-1:]]

    lower_partner = partner[:half] - half
    uppers = jnp.arange(half, dtype=jnp.int32)
    pick = (lower_partner[:, None] == uppers[None, :]).astype(bf16)
    spread = pick.T

    wide = pltpu.VMEM((tiles, bonds * mom_local, LANES), jnp.float32)
    square = (half, half)
    matmul = 2 * mom_local * bonds**3
    field_bytes = 2 * mom_local * bonds * bonds
    field = jax.ShapeDtypeStruct(vertex.shape, bf16)
    token_shape = jax.ShapeDtypeStruct((8, LANES), jnp.float32)

    def flow(members):
        return jax.ShapeDtypeStruct((places, members, 2, group, mom_local, bonds), bf16)

    def one_flow():
        return pl.BlockSpec((places, 1, 2, group, mom_local, bonds), lambda c, i: (0, c, 0, 0, 0, 0))

    def matrix_at(start):
        return pl.BlockSpec((1, 1, bonds, bonds), lambda c, i: (c + start, i, 0, 0))

    def exchange(outgoing):
        return lax.all_to_all(outgoing, AXES, split_axis=0, concat_axis=0, tiled=True)

    pair = PAIR if mom_local % PAIR == 0 else 1
    plain = jax.ShapeDtypeStruct((places, 1, mom_local, 2, group, bonds), bf16)
    plain_block = pl.BlockSpec((places, 1, pair, 2, group, bonds), lambda i: (0, 0, i, 0, 0, 0))

    def pair_at(start):
        return pl.BlockSpec((1, pair, bonds, bonds), lambda i: (start, i, 0, 0))

    base, outgoing, token = pl.pallas_call(
        functools.partial(first_product_kernel, places),
        grid=(mom_local // pair,),
        in_specs=[pair_at(0), pair_at(0), whole(square), whole(square)],
        out_specs=[pair_at(0), plain_block, whole(token_shape.shape)],
        out_shape=[field, plain, token_shape],
        compiler_params=params(1),
        cost_estimate=pl.CostEstimate(flops=5 * matmul // 2, bytes_accessed=4 * field_bytes, transcendentals=0),
        name="product_first",
    )(vertex, loop_matrix, pick, spread)
    whole_rows = with_layout_constraint(exchange(outgoing), Layout(major_to_minor=tuple(range(6))))
    arrived = [whole_rows.transpose(0, 1, 3, 4, 2, 5)]
    for members in send_groups[1:]:
        matrix = matrix_at(members[0])
        size = len(members)
        base, outgoing, _ = pl.pallas_call(
            functools.partial(product_kernel, mom_local, places),
            grid=(size, mom_local),
            in_specs=[matrix, matrix, whole(square), whole(square)]
            + [pl.BlockSpec(memory_space=pl.ANY)],
            out_specs=[matrix, one_flow(), whole(token_shape.shape)],
            out_shape=[field, flow(size), token_shape],
            input_output_aliases={4: 0},
            scratch_shapes=[wide],
            compiler_params=params(2),
            cost_estimate=pl.CostEstimate(
                flops=5 * size * matmul // 2, bytes_accessed=4 * size * field_bytes, transcendentals=0
            ),
            name="product_%d" % members[0],
        )(vertex, loop_matrix, pick, spread, base)
        arrived.append(exchange(outgoing))

    shells, partner, grid_index, own_mix, cross_mix, _ = lax.optimization_barrier(
        (shells, partner, grid_index, own_mix, cross_mix, token)
    )
    plus_table = cas_table(grid_index, False)
    minus_table = cas_table(grid_index, True)
    back_table = plus_table.T
    cycle = cycle_index(count)[:, None]
    shell_order = jnp.concatenate([shells[:half], jnp.take(shells, partner[:half])])
    shell_rows = lax.dynamic_slice_in_dim(shell_order.reshape(2, half), place * group, group, axis=1)
    reach = (shell_rows[:, :, None] + shell_order[None, None, :]).reshape(2, group, 1, bonds)
    own_scaled = own_mix * (1.0 / count)
    cross_scaled = cross_mix * (1.0 / count)

    rows = ROWS if group % ROWS == 0 else 1

    def row_block(members):
        return pl.BlockSpec((places, members, 2, rows, mom_local, bonds), lambda i: (0, 0, 0, i, 0, 0))

    table = whole((count, count))
    scalars = pl.BlockSpec(memory_space=pltpu.SMEM)
    sizes = [len(members) for members in send_groups]
    finished, earlier = [], []
    for members in back_groups:
        size = len(members)
        outgoing = pl.pallas_call(
            functools.partial(lattice_kernel, sizes, members),
            grid=(group // rows,),
            in_specs=[
                scalars,
                scalars,
                table,
                table,
                table,
                whole((count, 1)),
                pl.BlockSpec((2, rows, 1, bonds), lambda i: (0, i, 0, 0)),
            ]
            + [row_block(n) for n in sizes]
            + [pl.BlockSpec(memory_space=pl.ANY)] * len(earlier),
            out_specs=row_block(size),
            out_shape=flow(size),
            compiler_params=params(1),
            cost_estimate=pl.CostEstimate(
                flops=(2 * channels + size) * 2 * count * count * 2 * group * bonds,
                bytes_accessed=(channels + size) * field_bytes,
                transcendentals=0,
            ),
            name="lattice_%d" % members[0],
        )(own_scaled, cross_scaled, plus_table, minus_table, back_table, cycle, reach, *arrived, *earlier)
        earlier = [outgoing]
        if members is back_groups[-1]:
            outgoing = outgoing.transpose(0, 1, 4, 2, 3, 5)
        finished.append(exchange(outgoing))

    for members, received in zip(back_groups[:-1], finished[:-1]):
        matrix = matrix_at(members[0])
        size = len(members)
        base = pl.pallas_call(
            functools.partial(finish_kernel, mom_local),
            grid=(size, mom_local),
            in_specs=[matrix, one_flow(), whole(square), whole(square)],
            out_specs=matrix,
            out_shape=field,
            input_output_aliases={0: 0},
            scratch_shapes=[wide],
            compiler_params=params(2),
            cost_estimate=pl.CostEstimate(
                flops=size * matmul // 2, bytes_accessed=3 * size * field_bytes, transcendentals=0
            ),
            name="finish_%d" % members[0],
        )(base, received, pick, spread)
    last = back_groups[-1][0]
    return pl.pallas_call(
        last_finish_kernel,
        grid=(mom_local // pair,),
        in_specs=[pair_at(last), plain_block, whole(square), whole(square)],
        out_specs=pair_at(last),
        out_shape=field,
        input_output_aliases={0: 0},
        compiler_params=params(1),
        cost_estimate=pl.CostEstimate(flops=matmul // 2, bytes_accessed=3 * field_bytes, transcendentals=0),
        name="finish_last",
    )(base, finished[-1], pick, spread)


MESH = pl.DeviceIdType.MESH
FLOW_LIMIT = 44 * 1024 * 1024
LAST_LIMIT = 16 * 1024 * 1024


def flow_kernel(
    parts,
    vertex_ref,
    loop_ref,
    own_ref,
    cross_ref,
    partner_ref,
    shells_ref,
    grid_ref,
    base_ref,
    back_ref,
    tail_ref,
    send_ref,
    recv_ref,
    wide_ref,
    vertex_buf,
    loop_buf,
    pick_ref,
    spread_ref,
    block_ref,
    plus_ref,
    minus_ref,
    turn_ref,
    cycle_ref,
    row_ref,
    col_ref,
    load_sem,
    self_sem,
    out_sem,
    in_sem,
    home_sem,
    finish_sem,
):
    bf16, f32 = jnp.bfloat16, jnp.float32
    chunks, channels, places, depth, width = send_ref.shape
    mom_local, bonds = vertex_ref.shape[1], vertex_ref.shape[-1]
    half, count = bonds // 2, places * mom_local
    group = half // places
    pair = 2 * group
    side = math.isqrt(count)
    steps = channels * mom_local
    columns = lax.axis_size("bond")
    place = lax.axis_index("mom") * columns + lax.axis_index("bond")

    def device(offset):
        at = lax.rem(place + offset, places)
        return at, (lax.div(at, columns), lax.rem(at, columns))

    barrier = pltpu.get_barrier_semaphore()

    def greet(offset, carry):
        far = lax.rem(offset + places // 2 - 2, places - 1) + 1
        pl.semaphore_signal(barrier, inc=1, device_id=device(far)[1], device_id_type=MESH)
        return carry

    def loads(step, slot):
        c, n = lax.div(step, mom_local), lax.rem(step, mom_local)
        return [
            pltpu.make_async_copy(source.at[c, n], target.at[slot], load_sem.at[k, slot])
            for k, (source, target) in enumerate(((vertex_ref, vertex_buf), (loop_ref, loop_buf)))
        ]

    for copy in loads(0, 0):
        copy.start()
    lax.fori_loop(1, places, greet, 0)
    down = lax.broadcasted_iota(jnp.int32, (half, half), 0)
    lower_partner = partner_ref[:, :half] - half
    pick_ref[...] = jnp.where(down == partner_ref[:, half:], 1.0, 0.0).astype(bf16)
    spread_ref[...] = jnp.where(down == lower_partner, 1.0, 0.0).astype(bf16)

    def forward(unit_k, unit_c, first, size):
        unit = unit_k * channels + unit_c

        def one(offset, carry):
            at, target = device(offset)
            rows = pl.ds(first, size)
            pltpu.make_async_remote_copy(
                src_ref=send_ref.at[unit_k, unit_c, at, rows],
                dst_ref=recv_ref.at[unit_k, unit_c, place, rows],
                send_sem=out_sem.at[0, unit],
                recv_sem=in_sem.at[0, unit],
                device_id=target,
                device_id_type=MESH,
            ).start()
            return carry

        lax.fori_loop(1, places, one, 0)

    def backward(unit_k, unit_c, landing):
        unit = unit_k * channels + unit_c

        def one(offset, carry):
            at, target = device(offset)
            pltpu.make_async_remote_copy(
                src_ref=send_ref.at[unit_k, unit_c, at],
                dst_ref=landing.at[place],
                send_sem=out_sem.at[1, unit],
                recv_sem=in_sem.at[1, unit],
                device_id=target,
                device_id_type=MESH,
            ).start()
            return carry

        lax.fori_loop(1, places, one, 0)

    def landing_of(way, unit_k, unit_c):
        if way == 2:
            return tail_ref
        return (back_ref if way else recv_ref).at[unit_k, unit_c]

    def all_of(way, unit_k, unit_c):
        unit = unit_k * channels + unit_c
        return pltpu.make_async_remote_copy(
            src_ref=send_ref.at[unit_k, unit_c, pl.ds(0, places - 1)],
            dst_ref=landing_of(way, unit_k, unit_c).at[pl.ds(0, places - 1)],
            send_sem=out_sem.at[min(way, 1), unit],
            recv_sem=in_sem.at[min(way, 1), unit],
            device_id=device(1)[1],
            device_id_type=MESH,
        )

    def own_block(way, unit_k, unit_c):
        unit = unit_k * channels + unit_c
        return pltpu.make_async_copy(
            send_ref.at[unit_k, unit_c, place],
            landing_of(way, unit_k, unit_c).at[place],
            (home_sem if way else self_sem).at[unit],
        )

    part = mom_local // parts

    def product_step(step, carry):
        slot = lax.rem(step, 2)
        c, n = lax.div(step, mom_local), lax.rem(step, mom_local)

        @pl.when(step + 1 < steps)
        def _():
            for copy in loads(step + 1, 1 - slot):
                copy.start()

        for copy in loads(step, slot):
            copy.wait()
        vertex = vertex_buf[slot]
        half_product = dot(vertex, loop_buf[slot]).astype(bf16)
        product = dot(half_product, vertex)
        rounded = product.astype(bf16)
        left = rounded[:, :half]
        right = dot(rounded[:, half:], spread_ref[...]).astype(bf16)
        rows = pl.ds(pl.multiple_of(n * pair, pair), pair)
        for at, piece in enumerate((left, right)):
            upper = dot(pick_ref[...], piece[half:])
            lower = piece[:half].astype(f32)
            for k in range(chunks):
                cols = slice(k * LANES, (k + 1) * LANES)
                both = jnp.concatenate(
                    [lower[:, cols].reshape(places, group, LANES), upper[:, cols].reshape(places, group, LANES)], axis=1
                )
                send_ref[k, c, :, rows, at * LANES : (at + 1) * LANES] = both.astype(bf16)

        base_ref[c, n] = (product + vertex.astype(f32)).astype(bf16)

        @pl.when(step == part - 1)
        def _():
            pl.semaphore_wait(barrier, places - 1)

        @pl.when((c == 0) & (lax.rem(n, part) == part - 1))
        def _():
            forward(0, 0, pl.multiple_of((n - part + 1) * pair, part * pair), part * pair)

        @pl.when((c > 0) & (n == mom_local - 1))
        def _():
            forward(0, c, 0, depth)

        return carry

    lax.fori_loop(0, steps, product_step, 0)

    def later_chunk(unit, carry):
        forward(lax.div(unit, channels), lax.rem(unit, channels), 0, depth)
        return carry

    lax.fori_loop(channels, chunks * channels, later_chunk, 0)

    def start_own(unit, carry):
        own_block(0, lax.div(unit, channels), lax.rem(unit, channels)).start()
        return carry

    lax.fori_loop(0, chunks * channels, start_own, 0)

    def floor_div(value, by):
        return jnp.floor((value + 0.5) * (1.0 / by))

    points = lax.broadcasted_iota(jnp.int32, (count, count), 0).astype(f32)
    disp_x = floor_div(points, side)
    disp_y = points - side * disp_x
    far = []
    for disp in (disp_x, disp_y):
        moved = disp + side // 2
        far.append(jnp.abs(moved - side * floor_div(moved, side) - side // 2))
    cycle_ref[...] = jnp.maximum(far[0], far[1])
    grid = grid_ref[...].astype(f32)
    wave_x = floor_div(grid, side)
    wave_y = grid - side * wave_x
    phases = disp_x * wave_x + disp_y * wave_y
    phases = phases - side * floor_div(phases, side)
    angles = np.arange(side, dtype=np.float32) * np.float32(2.0 * math.pi / side)
    cas = (np.cos(angles) + np.sin(angles)).astype(np.float32)
    plus = jnp.zeros_like(phases)
    minus = jnp.zeros_like(phases)
    for phase in range(side):
        here = phases == float(phase)
        plus = jnp.where(here, float(cas[phase]), plus)
        minus = jnp.where(here, float(cas[(side - phase) % side]), minus)
    plus_ref[...] = plus.astype(bf16)
    minus_ref[...] = minus.astype(bf16)
    turn_ref[...] = plus.T.astype(bf16)

    shells = shells_ref[...].astype(f32)
    low_shells = shells[:, :half]
    up_shells = dot(jnp.broadcast_to(shells[:, half:], (8, half)).astype(bf16), spread_ref[...])[:1]
    lane = lax.broadcasted_iota(jnp.int32, (group, half), 1)
    mine = lane == place * group + lax.broadcasted_iota(jnp.int32, (group, half), 0)
    for s, line in enumerate((low_shells, up_shells)):
        column = jnp.sum(jnp.where(mine, jnp.broadcast_to(line, (group, half)), 0.0), axis=1, keepdims=True)
        row_ref[s * group : (s + 1) * group] = jnp.broadcast_to(column, (group, width))
        for k in range(chunks):
            cols = slice(k * LANES, (k + 1) * LANES)
            col_ref[k, :, s * LANES : (s + 1) * LANES] = jnp.broadcast_to(line[:, cols], (8, LANES))
    for k in range(chunks):
        cols = slice(k * LANES, (k + 1) * LANES)
        block_ref[k] = pick_ref[cols, cols]

    def lattice_chunk(k, carry):
        for c in range(channels):
            all_of(0, k, c).wait_recv()
            own_block(0, k, c).wait()

        def widen(at, carry):
            for c in range(channels):
                rows = pl.ds(pl.multiple_of(at * depth, depth), depth)
                block = recv_ref[k, c, at].astype(f32)
                for t in range(2):
                    wide_ref[c, t, rows] = block[:, t * LANES : (t + 1) * LANES]
            return carry

        lax.fori_loop(0, places, widen, 0)

        def row_step(i, carry):
            def lines(s):
                return pl.ds(s * group + i, count, stride=pair)

            blocks = [
                [
                    jnp.concatenate([wide_ref[c, t, lines(s)] for t in range(2)], axis=1).astype(bf16)
                    for s in range(2)
                ]
                for c in range(channels)
            ]
            for s in range(2):
                mixed = [None] * channels
                for c in range(channels):
                    own = dot(plus_ref[...], blocks[c][s])
                    crossed = dot(minus_ref[...], blocks[c][1 - s])
                    crossed = jnp.concatenate([crossed[:, LANES:], crossed[:, :LANES]], axis=1)
                    for d in range(channels):
                        term = own_ref[d, c] * own + cross_ref[d, c] * crossed
                        mixed[d] = term if c == 0 else mixed[d] + term
                reach = row_ref[pl.ds(s * group + i, 1)] + col_ref[k, :1]
                kept = cycle_ref[:, :width] <= reach
                for d in range(channels):
                    projected = jnp.where(kept, mixed[d] * (1.0 / count), 0.0).astype(bf16)
                    returned = dot(turn_ref[...], projected)
                    for t in range(2):
                        wide_ref[d, t, lines(s)] = returned[:, t * LANES : (t + 1) * LANES]
            return carry

        lax.fori_loop(0, group, row_step, 0)
        for c in range(channels):
            all_of(0, k, c).wait_send()

        def narrow(at, carry):
            for d in range(channels):
                rows = pl.ds(pl.multiple_of(at * depth, depth), depth)
                block = jnp.concatenate([wide_ref[d, t, rows] for t in range(2)], axis=1)
                send_ref[k, d, at] = block.astype(bf16)
            return carry

        lax.fori_loop(0, places, narrow, 0)
        for d in range(channels - 1):
            backward(k, d, back_ref.at[k, d])
            own_block(1, k, d).start()

        @pl.when(k < chunks - 1)
        def _():
            backward(k, channels - 1, back_ref.at[k, channels - 1])
            own_block(1, k, channels - 1).start()

        @pl.when(k == chunks - 1)
        def _():
            backward(k, channels - 1, tail_ref)
            own_block(2, k, channels - 1).start()

        return carry

    lax.fori_loop(0, chunks, lattice_chunk, 0)

    def finish_unit(unit, carry):
        k, d = lax.div(unit, channels), lax.rem(unit, channels)
        all_of(1, k, d).wait_recv()
        own_block(1, k, d).wait()
        arrival = pltpu.make_async_copy(back_ref.at[k, d], recv_ref.at[0, 0], finish_sem)
        arrival.start()
        arrival.wait()

        def finish_matrix(n, carry):
            rows = pl.ds(pl.multiple_of(n * pair, pair), pair)
            block = recv_ref[0, 0, :, rows].astype(f32)
            for s in range(2):
                there = slice(s * half, (s + 1) * half)
                piece = block[:, s * group : (s + 1) * group].reshape(half, width)
                if s:
                    piece = dot(spread_ref[...], piece.astype(bf16))
                right = dot(piece[:, LANES:].astype(bf16), block_ref[k])
                for t, add in enumerate((piece[:, :LANES], right)):
                    cols = pl.ds(pl.multiple_of(k * LANES + t * half, LANES), LANES)
                    base_ref[d, n, there, cols] = (base_ref[d, n, there, cols].astype(f32) + add).astype(bf16)
            return carry

        lax.fori_loop(0, mom_local, finish_matrix, 0)
        return carry

    units = chunks * channels
    lax.fori_loop(0, units - 1, finish_unit, 0)
    all_of(2, chunks - 1, channels - 1).wait_recv()
    own_block(2, chunks - 1, channels - 1).wait()

    def drain(unit, carry):
        all_of(1, lax.div(unit, channels), lax.rem(unit, channels)).wait_send()
        return carry

    lax.fori_loop(0, units, drain, 0)


def last_kernel(base_ref, block_ref, partner_ref, out_ref, tile_ref, pass_sem, out_sem):
    bf16, f32 = jnp.bfloat16, jnp.float32
    places, _, width = block_ref.shape
    channels, mom_local, bonds = base_ref.shape[:3]
    half = bonds // 2
    chunks = half // LANES
    group = half // places
    pair = 2 * group
    d, edge = channels - 1, (chunks - 1) * LANES
    done = [(base_ref.at[pl.ds(0, d)], out_ref.at[pl.ds(0, d)])] if d else []
    passing = [pltpu.make_async_copy(*ends, pass_sem.at[at]) for at, ends in enumerate(done)]
    for copy in passing:
        copy.start()
    down = lax.broadcasted_iota(jnp.int32, (half, half), 0)
    spread = jnp.where(down == partner_ref[:, :half] - half, 1.0, 0.0).astype(bf16)
    pick = jnp.where(down[:LANES, :LANES] + edge == partner_ref[:, half + edge :], 1.0, 0.0).astype(bf16)
    leaving = []
    for n in range(mom_local):
        block = block_ref[:, n * pair : (n + 1) * pair].astype(f32)
        for s in range(2):
            there = slice(s * half, (s + 1) * half)
            piece = block[:, s * group : (s + 1) * group].reshape(half, width)
            if s:
                piece = dot(spread, piece.astype(bf16))
            right = dot(piece[:, LANES:].astype(bf16), pick)
            for t, add in enumerate((piece[:, :LANES], right)):
                cols = slice(t * half + edge, t * half + edge + LANES)
                tile_ref[n, there, cols] = (base_ref[d, n, there, cols].astype(f32) + add).astype(bf16)
                if edge:
                    kept = slice(t * half, t * half + edge)
                    tile_ref[n, there, kept] = base_ref[d, n, there, kept]
        copy = pltpu.make_async_copy(tile_ref.at[n], out_ref.at[d, n], out_sem.at[n])
        copy.start()
        leaving.append(copy)
    for copy in passing + leaving:
        copy.wait()


def chunked_flow(vertex, loop_matrix, own_mix, cross_mix, shells, partner, grid_index):
    places = lax.axis_size("mom") * lax.axis_size("bond")
    channels, mom_local, bonds, _ = vertex.shape
    count = grid_index.shape[0]
    half = bonds // 2
    group = half // places
    chunks = half // LANES
    width = 2 * LANES
    depth = mom_local * 2 * group
    units = chunks * channels
    bf16, f32 = jnp.bfloat16, jnp.float32
    parts = mom_local // PAIR if mom_local % PAIR == 0 else 1
    anywhere = pl.BlockSpec(memory_space=pl.ANY)
    scalars = pl.BlockSpec(memory_space=pltpu.SMEM)
    inside = pl.BlockSpec(memory_space=pltpu.VMEM)
    dma = pltpu.SemaphoreType.DMA
    base, _, tail = pl.pallas_call(
        functools.partial(flow_kernel, parts),
        in_specs=[anywhere, anywhere, scalars, scalars, inside, inside, inside],
        out_specs=[inside, anywhere, inside],
        out_shape=[
            pltpu.VMEM(vertex.shape, bf16),
            pltpu.HBM((chunks, channels, places, depth, width), bf16),
            pltpu.VMEM((places, depth, width), bf16),
        ],
        scratch_shapes=[
            pltpu.VMEM((chunks, channels, places, depth, width), bf16),
            pltpu.VMEM((chunks, channels, places, depth, width), bf16),
            pltpu.VMEM((channels, 2, places * depth, LANES), f32),
            pltpu.VMEM((2, bonds, bonds), bf16),
            pltpu.VMEM((2, bonds, bonds), bf16),
            pltpu.VMEM((half, half), bf16),
            pltpu.VMEM((half, half), bf16),
            pltpu.VMEM((chunks, LANES, LANES), bf16),
            pltpu.VMEM((count, count), bf16),
            pltpu.VMEM((count, count), bf16),
            pltpu.VMEM((count, count), bf16),
            pltpu.VMEM((count, count), f32),
            pltpu.VMEM((2 * group, width), f32),
            pltpu.VMEM((chunks, 8, width), f32),
            dma((2, 2)),
            dma((units,)),
            dma((2, units)),
            dma((2, units)),
            dma((units,)),
            dma(()),
        ],
        compiler_params=pltpu.CompilerParams(collective_id=0, has_side_effects=True, vmem_limit_bytes=FLOW_LIMIT),
        name="flow",
    )(
        vertex,
        loop_matrix,
        own_mix,
        cross_mix,
        partner.reshape(1, bonds),
        shells.reshape(1, bonds),
        grid_index.reshape(1, count),
    )

    return pl.pallas_call(
        last_kernel,
        in_specs=[inside, inside, inside],
        out_specs=anywhere,
        out_shape=pltpu.HBM(vertex.shape, bf16),
        scratch_shapes=[
            pltpu.VMEM((mom_local, bonds, bonds), bf16),
            dma((channels,)),
            dma((mom_local,)),
        ],
        compiler_params=pltpu.CompilerParams(vmem_limit_bytes=LAST_LIMIT),
        name="finish_last_unit",
    )(base, tail, partner.reshape(1, bonds))


def per_device(vertex, *others):
    places = lax.axis_size("mom") * lax.axis_size("bond")
    half = vertex.shape[-1] // 2
    group = half // places
    if group and group % 8 == 0 and half % LANES == 0 and places * vertex.shape[1] >= 2 * LANES:
        return chunked_flow(vertex, *others)
    return general_flow(vertex, *others)


def solution(mesh):
    in_specs = (P(None, AXES, None, None), P(None, AXES, None, None), P(), P(), P(), P(), P())
    return jax.shard_map(
        per_device, mesh=mesh, in_specs=in_specs, out_specs=P(None, AXES, None, None), check_vma=False
    )
```
